32 devices in a mesh: wide: 16 (over z, y, core), shard: 2 (over x).
Axes of the slice: x: 2, y: 2, z: 4, core: 2. Of those that a mesh axis runs over, the one named last changes fastest.
Arguments:
- weights: bfloat16 [256, 8192], P('shard'), may hold values from -6 to 6
- momentum: bfloat16 [16, 256, 8192], P('wide', 'shard'), may hold values from -6 to 6
- grads: bfloat16 [2, 16, 256, 8192], P(None, 'wide', 'shard'), may hold values from -6 to 6
- offsets: int32 [2, 64], P('shard'), may hold values from 0 to 96
- owners: int32 [2, 64], P('shard'), may hold values from 0 to 63, each once within a row
- exp_avg: float32 [2, 64, 32, 128], P('shard', 'wide'), may hold values from -7 to 7
- exp_sq: float32 [2, 64, 32, 128], P('shard', 'wide'), may hold values from 0.01 to 1
Outputs:
- new_weights: bfloat16 [256, 8192], P('shard')
- new_momentum: bfloat16 [16, 256, 8192], P('wide', 'shard')
- new_avg: float32 [2, 64, 32, 128], P('shard', 'wide')
- new_sq: float32 [2, 64, 32, 128], P('shard', 'wide')
- scales: float32 [2], replicated
The draws below stay inside these ranges and needn't reach their ends.
Inputs may be any that keep to these rules, and one draw needn't show every extreme that they name: `offsets`: each block's band spans 32 consecutive transform rows. Each row of owners is a permutation of 0 to 63.
All inputs are finite; a program needn't handle non-finite values.
Results may differ from the reference program's by a relative error of at most 0.003.
Values may be sent and summed in bfloat16 or wider, within the bound.
No kernel may reach another device: no remote copies, remote signals or barrier semaphores. Data moves between devices by JAX's collectives and lax.ppermute only.
A program may use at most 128 MiB of HBM per device.

```python
import math
import jax
import jax.numpy as jnp
from jax import lax

BLOCK = 128
BAND = 32
COLS = 8192
STEPS = 2
ROW_BLOCKS = 2
ROWS = 256
CB = 64
REPLICAS = 16


def draw_exp_avg(key, part):
    array_shape = (ROW_BLOCKS, CB, BAND, BLOCK)
    row_pos = jnp.arange(ROW_BLOCKS, dtype=jnp.float32)[:, None, None, None] / max(ROW_BLOCKS - 1, 1)
    slot_pos = jnp.arange(CB, dtype=jnp.float32)[None, :, None, None] / max(CB - 1, 1)
    scaling = 0.15 * 3.0 ** (row_pos + slot_pos)
    base_draw = jnp.clip(jax.random.normal(key, array_shape, jnp.float32), -4.0, 4.0)
    return base_draw * scaling


def touch_ends(array, key, smallest, largest):
    extent = array.shape
    spot = [jax.random.randint(jax.random.fold_in(key, axis), (), 0, extent[axis]) for axis in range(len(extent))]
    array = array.at[tuple(spot)].set(smallest)
    longest = extent.index(max(extent))
    spot[longest] = (spot[longest] + 1) % extent[longest]
    return array.at[tuple(spot)].set(largest)


def raised(entries, key, source, target, parts, factor):
    owner, partner = [(jnp.arange(entries.shape[dim]) // (entries.shape[dim] // parts)).reshape([-1 if axis == dim else 1 for axis in range(entries.ndim)]) for dim in (source, target)]
    chosen = jax.random.permutation(key, parts)[partner]
    strong = (owner == chosen) | (owner == (partner + parts // 2) % parts)
    return jnp.where(strong, factor * entries, entries)


def steps_of(rng, dims, shards, low, high):
    loudness, own = 1.0, jax.random.fold_in(rng, 6)
    for dim, blocks in shards:
        draws = jnp.exp(jax.random.uniform(jax.random.fold_in(own, dim), (blocks,), jnp.float32, low / len(shards), high / len(shards)))
        loudness = loudness * jnp.repeat(draws, dims[dim] // blocks).reshape([-1 if axis == dim else 1 for axis in range(len(dims))])
    return loudness


def scatter_about(own_key, shape, deviation, bound, pieces=(), kind=jnp.bfloat16):
    entries = jax.random.normal(own_key, shape, jnp.float32) * deviation
    if len(pieces) > 0:
        entries = steps_of(own_key, shape, pieces, -0.22, 0.18) * entries
    return jnp.clip(entries, min=-bound, max=bound).astype(kind)


def heavy_noise(own_key, extent, scale, limit, pieces, heavy, kind=jnp.bfloat16):
    values = scale * jax.random.normal(own_key, extent, jnp.float32)
    if pieces:
        values = values * steps_of(own_key, extent, pieces, -0.22, 0.18)
    return jnp.clip(raised(values, jax.random.fold_in(own_key, 3), *heavy), -limit, limit).astype(kind)


def setup_inputs(seed: int = 0) -> dict:
    keys = jax.random.split(jax.random.key(seed), 8)
    return {
        "weights": scatter_about(keys[0], (ROWS, COLS), 1.0, 6.0, ((0, 2),)),
        "momentum": scatter_about(keys[1], (REPLICAS, ROWS, COLS), 1.0, 6.0, ((0, 16), (1, 2))),
        "grads": heavy_noise(keys[2], (STEPS, REPLICAS, ROWS, COLS), 1.0, 6.0, ((1, 16), (2, 2)), (1, 3, 16, 2.0)),
        "offsets": touch_ends(jax.random.randint(keys[3], (ROW_BLOCKS, CB), 0, BLOCK - BAND + 1), jax.random.fold_in(keys[3], 1), 0, BLOCK - BAND).astype(jnp.int32),
        "owners": jax.vmap(lambda own: jax.random.permutation(own, CB))(jax.random.split(keys[4], ROW_BLOCKS)).reshape((ROW_BLOCKS, CB)).astype(jnp.int32),
        "exp_avg": draw_exp_avg(jax.random.fold_in(keys[7], 71), 0),
        "exp_sq": jnp.clip(jnp.exp(math.log(1.0) - 4.6051702 * jax.random.uniform(keys[6], (ROW_BLOCKS, CB, BAND, BLOCK), jnp.float32) ** steps_of(keys[6], (ROW_BLOCKS, CB, BAND, BLOCK), ((0, 2), (1, 16)), -0.2, 0.2)), 0.01, 1.0),
    }


highest = lax.Precision.HIGHEST
momentum_decay = 0.9
beta_one = 0.8
beta_two = 0.95
adam_eps = 1e-08
rms_eps = 1e-06
learning_rate = 0.2

def dct_table(length):
    frequency = jnp.arange(length, dtype=jnp.float32)[:, None]
    position = jnp.arange(length, dtype=jnp.float32)[None, :]
    cosines = jnp.cos(jnp.pi * (2.0 * position + 1.0) * frequency / (2.0 * length))
    scaling = jnp.where(frequency == 0.0, jnp.sqrt(1.0 / length), jnp.sqrt(2.0 / length))
    return cosines * scaling

def band_tables(basis, offsets):
    indices = offsets[:, :, None] + jnp.arange(BAND, dtype=jnp.int32)[None, None, :]
    return basis[indices]

def forward(blended, picked, basis):
    left_part = jnp.einsum('rjpa,rajb->rjpb', picked, blended, precision=highest)
    return jnp.einsum('rjpb,cb->rjpc', left_part, basis, precision=highest)

def inverse(coefs, picked, basis):
    right_part = jnp.einsum('rjpc,cb->rjpb', coefs, basis, precision=highest)
    return jnp.einsum('rjpa,rjpb->rajb', picked, right_part, precision=highest)

def reference(weights, momentum, grads, offsets, owners, exp_avg, exp_sq):
    basis = dct_table(BLOCK)
    picked = band_tables(basis, offsets)
    slot_order = jnp.argsort(owners, axis=1).astype(jnp.int32)
    block_shape = (ROW_BLOCKS, BLOCK, CB, BLOCK)
    weight_now = weights.astype(jnp.float32).reshape(block_shape)
    moment_now = momentum.astype(jnp.float32).reshape((REPLICAS,) + block_shape)
    avg_now = exp_avg
    sq_now = exp_sq
    scales = []
    for step_index in range(STEPS):

        def one_replica(pair_in):
            held_moment, grad_now = pair_in
            blended = momentum_decay * held_moment + grad_now.astype(jnp.float32).reshape(block_shape)
            band_coef = forward(blended, picked, basis)
            return (band_coef, blended - inverse(band_coef, picked, basis))
        bands, moment_now = lax.map(one_replica, (moment_now, grads[step_index]))
        mean_band = lax.optimization_barrier(jnp.sum(bands, axis=0)) / REPLICAS
        slot_band = jnp.take_along_axis(mean_band, slot_order[:, :, None, None], axis=1)
        avg_now = beta_one * avg_now + (1.0 - beta_one) * slot_band
        sq_now = beta_two * sq_now + (1.0 - beta_two) * slot_band * slot_band
        raw_update = avg_now / (jnp.sqrt(sq_now) + adam_eps)
        spread = jnp.sqrt(jnp.mean(raw_update * raw_update) + rms_eps)
        update = (raw_update / spread).astype(jnp.bfloat16)
        block_update = jnp.take_along_axis(update.astype(jnp.float32), owners[:, :, None, None], axis=1)
        weight_now = weight_now - learning_rate * inverse(block_update, picked, basis)
        scales.append(spread)
    new_weights = weight_now.reshape(ROWS, COLS).astype(jnp.bfloat16)
    new_momentum = moment_now.reshape(REPLICAS, ROWS, COLS).astype(jnp.bfloat16)
    return (new_weights, new_momentum, avg_now, sq_now, jnp.stack(scales))
```

```python
import jax
import jax.numpy as jnp
import numpy as np
from jax import lax
from jax.experimental import pallas as pl
from jax.experimental.pallas import tpu as pltpu
from jax.sharding import PartitionSpec as P

STEPS = 2

momentum_decay = 0.9
beta_one = 0.8
beta_two = 0.95
adam_eps = 1e-08
rms_eps = 1e-06
learning_rate = 0.2


def dct_table(length):
    frequency = np.arange(length, dtype=np.float64)[:, None]
    position = np.arange(length, dtype=np.float64)[None, :]
    cosines = np.cos(np.pi * (2.0 * position + 1.0) * frequency / (2.0 * length))
    scaling = np.where(frequency == 0.0, np.sqrt(1.0 / length), np.sqrt(2.0 / length))
    return (cosines * scaling).astype(np.float32)


def halves(value):
    high = value.astype(jnp.bfloat16)
    return high, (value - high.astype(jnp.float32)).astype(jnp.bfloat16)


def dot(left, right):
    return jnp.dot(left, right, preferred_element_type=jnp.float32)


def slot_place(slot, device, replicas, row, row_blocks, owned):
    relative = (slot // owned) ^ device
    place = 0
    for bit in range(replicas.bit_length() - 1):
        place = place * 2 + ((relative >> bit) & 1)
    return (place * row_blocks + row) * owned + slot % owned


def forward_step(moment, grads, step_index, offsets, owners, table, replicas, moment_type, width):
    row_blocks, col_blocks = offsets.shape
    block_len = table.shape[0]
    band_rows = forward_step.band_rows
    columns = col_blocks * block_len
    owned = col_blocks // replicas
    slots = row_blocks * col_blocks
    half = slots // 2

    def kernel(offsets_ref, owners_ref, moment_ref, grads_ref, table_ref, turned_ref, moment_out, keep_out,
               send_out, scatter, coefs, held):
        row = pl.program_id(0)
        chunk = pl.program_id(1)
        device = lax.axis_index("wide")
        blended = momentum_decay * moment_ref[...].astype(jnp.float32) + grads_ref[0].astype(jnp.float32)
        blend_high, blend_low = halves(blended)
        scatter[...] = jnp.zeros_like(scatter)
        for index in range(width):
            offset = offsets_ref[row, chunk * width + index]
            lanes = slice(index * block_len, (index + 1) * block_len)
            pick_high, pick_low = halves(table_ref[pl.ds(offset, band_rows), :])
            both = dot(jnp.concatenate([pick_high, pick_low], 0), blend_high[:, lanes])
            left = both[:band_rows] + both[band_rows:] + dot(pick_high, blend_low[:, lanes])
            scatter[index, pl.ds(offset, band_rows), :] = left
            coefs[index * band_rows:(index + 1) * band_rows, :] = left
        turn_high, turn_low = halves(turned_ref[...])
        coef_high, coef_low = halves(coefs[...])
        band = dot(coef_high, turn_high) + dot(coef_high, turn_low) + dot(coef_low, turn_high)
        for index in range(width):
            slot = owners_ref[row, chunk * width + index]
            held[slot_place(slot, device, replicas, row, row_blocks, owned)] = band[
                index * band_rows:(index + 1) * band_rows]
        spread_high, spread_low = halves(jnp.concatenate([scatter[index] for index in range(width)], 1))
        inverse = dot(turn_high, spread_high) + dot(turn_low, spread_high) + dot(turn_high, spread_low)
        moment_out[...] = (blended - inverse).astype(moment_out.dtype)

        @pl.when((row == pl.num_programs(0) - 1) & (chunk == pl.num_programs(1) - 1))
        def _():
            keep_out[...] = held[:half]
            send_out[...] = held[half:].astype(send_out.dtype)

    tile = (block_len, width * block_len)
    whole = lambda row, chunk: (0, 0, 0)
    return pl.pallas_call(
        kernel,
        grid=(row_blocks, col_blocks // width),
        in_specs=[
            pl.BlockSpec(memory_space=pltpu.SMEM),
            pl.BlockSpec(memory_space=pltpu.SMEM),
            pl.BlockSpec(tile, lambda row, chunk: (row, chunk)),
            pl.BlockSpec((1,) + tile, lambda row, chunk: (step_index, row, chunk)),
            pl.BlockSpec(table.shape, lambda row, chunk: (0, 0)),
            pl.BlockSpec(table.shape, lambda row, chunk: (0, 0)),
        ],
        out_specs=[
            pl.BlockSpec(tile, lambda row, chunk: (row, chunk)),
            pl.BlockSpec((half, band_rows, block_len), whole),
            pl.BlockSpec((half, band_rows, block_len), whole),
        ],
        out_shape=[
            jax.ShapeDtypeStruct((row_blocks * block_len, columns), moment_type),
            jax.ShapeDtypeStruct((half, band_rows, block_len), jnp.float32),
            jax.ShapeDtypeStruct((half, band_rows, block_len), jnp.bfloat16),
        ],
        scratch_shapes=[
            pltpu.VMEM((width, block_len, block_len), jnp.float32),
            pltpu.VMEM((width * band_rows, block_len), jnp.float32),
            pltpu.VMEM((slots, band_rows, block_len), jnp.float32),
        ],
        name=f"forward_{step_index}",
    )(offsets, owners, moment, grads, table, table.T)


def weights_update(weights, near, far, scales, offsets, owners, table, replicas, width):
    row_blocks, col_blocks = offsets.shape
    block_len = table.shape[0]
    band_rows = forward_step.band_rows
    owned = col_blocks // replicas
    count = row_blocks * owned
    groups = replicas // 2

    def kernel(offsets_ref, owners_ref, scales_ref, weights_ref, near_ref, far_ref, table_ref, turned_ref, out_ref,
               scatter, updates):
        row = pl.program_id(0)
        chunk = pl.program_id(1)
        device = lax.axis_index("wide")
        scatter[...] = jnp.zeros_like(scatter)
        for index in range(width):
            slot = owners_ref[row, chunk * width + index]
            place = slot_place(slot, device, replicas, row, row_blocks, owned)
            group = place // count
            within = place % count
            remote = group >= groups
            group = jnp.where(remote, group - groups, group)
            total = 0.0
            for step_index in range(STEPS):
                entry = step_index * count + within
                raw = jnp.where(remote, far_ref[group, entry].astype(jnp.float32), near_ref[group, entry].astype(jnp.float32))
                total = total + raw / scales_ref[step_index]
            updates[index * band_rows:(index + 1) * band_rows, :] = total
        base_high, base_low = halves(table_ref[...])
        up_high, up_low = halves(updates[...])
        right = dot(up_high, base_high) + dot(up_high, base_low) + dot(up_low, base_high)
        for index in range(width):
            offset = offsets_ref[row, chunk * width + index]
            scatter[index, pl.ds(offset, band_rows), :] = right[index * band_rows:(index + 1) * band_rows]
        turn_high, turn_low = halves(turned_ref[...])
        spread_high, spread_low = halves(jnp.concatenate([scatter[index] for index in range(width)], 1))
        inverse = dot(turn_high, spread_high) + dot(turn_low, spread_high) + dot(turn_high, spread_low)
        out_ref[...] = (weights_ref[...].astype(jnp.float32) - learning_rate * inverse).astype(out_ref.dtype)

    tile = (block_len, width * block_len)
    whole = lambda row, chunk: (0, 0, 0, 0)
    return pl.pallas_call(
        kernel,
        grid=(row_blocks, col_blocks // width),
        in_specs=[
            pl.BlockSpec(memory_space=pltpu.SMEM),
            pl.BlockSpec(memory_space=pltpu.SMEM),
            pl.BlockSpec(memory_space=pltpu.SMEM),
            pl.BlockSpec(tile, lambda row, chunk: (row, chunk)),
            pl.BlockSpec(near.shape, whole),
            pl.BlockSpec(far.shape, whole),
            pl.BlockSpec(table.shape, lambda row, chunk: (0, 0)),
            pl.BlockSpec(table.shape, lambda row, chunk: (0, 0)),
        ],
        out_specs=pl.BlockSpec(tile, lambda row, chunk: (row, chunk)),
        out_shape=jax.ShapeDtypeStruct(weights.shape, weights.dtype),
        scratch_shapes=[
            pltpu.VMEM((width, block_len, block_len), jnp.float32),
            pltpu.VMEM((width * band_rows, block_len), jnp.float32),
        ],
        name="weights_update",
    )(offsets, owners, scales, weights, near, far, table, table.T)


def swap(value, mask, replicas):
    return lax.ppermute(value, "wide", [(index, index ^ mask) for index in range(replicas)])


def per_device(weights, momentum, grads, offsets, owners, exp_avg, exp_sq):
    row_blocks, owned, band_rows, block_len = exp_avg.shape
    forward_step.band_rows = band_rows
    replicas = lax.axis_size("wide")
    shards = lax.axis_size("shard")
    count_all = exp_avg.size * replicas * shards
    table = jnp.asarray(dct_table(block_len))
    width = 8
    masks = [1 << bit for bit in range(replicas.bit_length() - 1)]
    local_grads = grads[:, 0]
    moment, keep_0, send_0 = forward_step(
        momentum[0], local_grads, 0, offsets, owners, table, replicas, jnp.float32, width)
    moment, keep_1, send_1 = forward_step(
        moment, local_grads, 1, offsets, owners, table, replicas, momentum.dtype, width)
    kept = [keep_0, keep_1]
    sent = [send_0, send_1]
    for mask in masks:
        got = [swap(value, mask, replicas) for value in sent]
        sums = [a + b.astype(jnp.float32) for a, b in zip(kept, got)]
        middle = sums[0].shape[0] // 2
        kept = [value[:middle] for value in sums]
        sent = [value[middle:].astype(jnp.bfloat16) for value in sums]
    avg_now = exp_avg
    sq_now = exp_sq
    raws = []
    powers = []
    for total in sums:
        mean_band = total.reshape(exp_avg.shape) / replicas
        avg_now = beta_one * avg_now + (1.0 - beta_one) * mean_band
        sq_now = beta_two * sq_now + (1.0 - beta_two) * mean_band * mean_band
        raw = avg_now / (jnp.sqrt(sq_now) + adam_eps)
        powers.append(jnp.sum(raw * raw))
        raws.append(raw.astype(jnp.bfloat16).reshape((row_blocks * owned, band_rows, block_len)))
    near = jnp.concatenate(raws, 0)[None]
    power = jnp.broadcast_to(jnp.stack(powers)[:, None], (STEPS, block_len))
    for shift in range(1, shards):
        power = power + lax.ppermute(power, "shard", [(i, (i + shift) % shards) for i in range(shards)])
    for mask in reversed(masks):
        power = power + swap(power, mask, replicas)
        far = swap(near, mask, replicas)
        if mask > 1:
            near = jnp.concatenate([near, far], 0)
    scales = jnp.sqrt(power[:, 0] / count_all + rms_eps)
    new_weights = weights_update(weights, near, far, scales, offsets, owners, table, replicas, width)
    return (new_weights, moment[None], avg_now, sq_now, scales)


def solution(mesh):
    in_specs = (
        P("shard", None),
        P("wide", "shard", None),
        P(None, "wide", "shard", None),
        P("shard", None),
        P("shard", None),
        P("shard", "wide", None, None),
        P("shard", "wide", None, None),
    )
    out_specs = (
        P("shard", None),
        P("wide", "shard", None),
        P("shard", "wide", None, None),
        P("shard", "wide", None, None),
        P(),
    )
    return jax.shard_map(
        per_device, mesh=mesh, in_specs=in_specs, out_specs=out_specs, check_vma=False
    )
```

```python
import jax
import jax.numpy as jnp
import numpy as np
from jax import lax
from jax.experimental import pallas as pl
from jax.experimental.pallas import tpu as pltpu
from jax.sharding import PartitionSpec as P

STEPS = 2

momentum_decay = 0.9
beta_one = 0.8
beta_two = 0.95
adam_eps = 1e-08
rms_eps = 1e-06
learning_rate = 0.2


SMEM = pl.BlockSpec(memory_space=pltpu.SMEM)
VMEM = pl.BlockSpec(memory_space=pltpu.VMEM)
ANY = pl.BlockSpec(memory_space=pl.ANY)
HBM = pl.BlockSpec(memory_space=pltpu.HBM)
SMALL = pltpu.CompilerParams(vmem_limit_bytes=20 << 20)


def dct_table(length):
    frequency = np.arange(length, dtype=np.float64)[:, None]
    position = np.arange(length, dtype=np.float64)[None, :]
    cosines = np.cos(np.pi * (2.0 * position + 1.0) * frequency / (2.0 * length))
    scaling = np.where(frequency == 0.0, np.sqrt(1.0 / length), np.sqrt(2.0 / length))
    return (cosines * scaling).astype(np.float32)


def split_table(table):
    high = table.astype(jnp.bfloat16)
    low = (table - high.astype(np.float32)).astype(jnp.bfloat16)
    return high, low


def row_tables(table):
    high, low = split_table(table)
    decayed_high, decayed_low = split_table(np.float32(momentum_decay) * table)
    wide = table.astype(np.float64)
    residue = momentum_decay * (np.eye(len(table)) - wide @ wide.T)
    parts = (high, low, decayed_high, decayed_low, residue.astype(np.float32).astype(jnp.bfloat16))
    return np.stack([part.astype(np.float32) for part in parts])


def column_tables(table):
    return np.stack([*split_table(table), *split_table(table.T)])


def near_memory(value):
    return pltpu.with_memory_space_constraint(value, pltpu.VMEM)


def far_memory(value):
    return pltpu.with_memory_space_constraint(value, pltpu.HBM)


def halves(value):
    high = value.astype(jnp.bfloat16)
    return high, (value - high.astype(jnp.float32)).astype(jnp.bfloat16)


def dot(left, right):
    return jnp.dot(left, right, preferred_element_type=jnp.float32)


def right_dot(left, high, low):
    left_high, left_low = halves(left)
    return dot(left_high, low) + (dot(left_high, high) + dot(left_low, high))


def slot_place(slot, device, order, row, row_blocks, owned):
    relative = (slot // owned) ^ device
    place = 0
    for bit in order:
        place = place * 2 + ((relative >> bit) & 1)
    return (place * row_blocks + row) * owned + slot % owned


def bands(momentum, grads, offsets, owners, picks, columns, band_rows, orders, width):
    row_blocks, col_blocks = offsets.shape
    block_len = picks.shape[-1]
    owned = col_blocks >> len(orders[0])
    slots = row_blocks * col_blocks
    half = slots // 2
    chunks = col_blocks // width
    span = width * block_len

    def kernel(offsets_hbm, owners_hbm, momentum_hbm, grads_hbm, picks_hbm, columns_hbm, momentum_ref, grads_ref, taken_ref,
               *refs):
        keep_refs, send_refs = refs[:STEPS], refs[STEPS:2 * STEPS]
        offsets_ref, owners_ref, picks_ref, columns_ref, scatter, lefts, tables, arrivals = refs[2 * STEPS:]
        device = lax.axis_index("wide")
        small = [
            pltpu.make_async_copy(source, target, tables.at[index])
            for index, (source, target) in enumerate([
                (offsets_hbm, offsets_ref), (owners_hbm, owners_ref), (picks_hbm, picks_ref), (columns_hbm, columns_ref)])
        ]
        for copy in small:
            copy.start()
        parts = [(row, chunk) for row in range(row_blocks) for chunk in range(chunks)]
        large = []
        for number, (row, chunk) in enumerate(parts):
            rows = slice(row * block_len, (row + 1) * block_len)
            lanes = slice(chunk * span, (chunk + 1) * span)
            large.append([
                pltpu.make_async_copy(momentum_hbm.at[rows, lanes], momentum_ref.at[rows, lanes], arrivals.at[0, number]),
                pltpu.make_async_copy(grads_hbm.at[:, rows, lanes], grads_ref.at[:, rows, lanes], arrivals.at[1, number]),
            ])
            for copy in large[-1]:
                copy.start()
        scatter[...] = jnp.zeros_like(scatter)
        for copy in small:
            copy.wait()
        for number, (row, chunk) in enumerate(parts):
            for copy in large[number]:
                copy.wait()
            base = number * width
            block_rows = slice(row * block_len, (row + 1) * block_len)
            for index in range(width):
                block = chunk * width + index
                rows = pl.ds(offsets_ref[row, block], band_rows)
                lanes = slice(block * block_len, (block + 1) * block_len)
                high, low, decayed_high, decayed_low, residue = [
                    picks_ref[part, rows, :].astype(jnp.bfloat16) for part in range(5)]
                first = jnp.concatenate(
                    [jnp.concatenate([decayed_high, high], 1), jnp.concatenate([decayed_low, low], 1)], 0)
                pair = dot(first, jnp.concatenate([momentum_ref[block_rows, lanes], grads_ref[0, block_rows, lanes]], 0))
                left_0 = pair[:band_rows] + pair[band_rows:]
                scatter[base + index, rows, :] = left_0
                second = jnp.concatenate(
                    [jnp.concatenate([high, residue], 1), jnp.concatenate([low, jnp.zeros_like(low)], 1)], 0)
                pair = dot(second, jnp.concatenate(
                    [grads_ref[1, block_rows, lanes], scatter[base + index].astype(jnp.bfloat16)], 0))
                left_1 = pair[:band_rows] + pair[band_rows:]
                begin = (STEPS * base + index) * band_rows
                lefts[begin:begin + band_rows, :] = left_0
                begin = (STEPS * base + width + index) * band_rows
                lefts[begin:begin + band_rows, :] = left_1
                begin = (base + index) * band_rows
                taken_ref[begin:begin + band_rows, :] = momentum_decay * left_0 + left_1
            begin = STEPS * base * band_rows
            band = right_dot(lefts[begin:begin + STEPS * width * band_rows, :], columns_ref[2], columns_ref[3])
            for index in range(width):
                slot = owners_ref[row, chunk * width + index]
                for step_index, order in enumerate(orders):
                    place = slot_place(slot, device, order, row, row_blocks, owned)
                    near = jnp.where(place < half, place, half)
                    far = jnp.where(place < half, half, place - half)
                    begin = (step_index * width + index) * band_rows
                    value = band[begin:begin + band_rows]
                    keep_refs[step_index][near] = value
                    send_refs[step_index][far] = value.astype(jnp.bfloat16)

    shape = (half + 1, band_rows, block_len)
    return pl.pallas_call(
        kernel,
        in_specs=[HBM] * 6,
        out_specs=[VMEM] * (3 + 2 * STEPS),
        out_shape=[
            pltpu.VMEM(momentum.shape, momentum.dtype),
            pltpu.VMEM(grads.shape, grads.dtype),
            pltpu.VMEM((slots * band_rows, block_len), jnp.float32),
        ] + [pltpu.VMEM(shape, jnp.float32)] * STEPS + [pltpu.VMEM(shape, jnp.bfloat16)] * STEPS,
        scratch_shapes=[
            pltpu.SMEM(offsets.shape, offsets.dtype),
            pltpu.SMEM(owners.shape, owners.dtype),
            pltpu.VMEM(picks.shape, picks.dtype),
            pltpu.VMEM(columns.shape, columns.dtype),
            pltpu.VMEM((slots, block_len, block_len), jnp.float32),
            pltpu.VMEM((STEPS * slots * band_rows, block_len), jnp.float32),
            pltpu.SemaphoreType.DMA((4,)),
            pltpu.SemaphoreType.DMA((2, row_blocks * chunks)),
        ],
        compiler_params=SMALL,
        name="bands",
    )(*map(far_memory, (offsets, owners, momentum, grads, picks, columns)))


def place_rows(scatters, index, rows, value):
    high = value.astype(jnp.bfloat16).astype(jnp.float32)
    scatters[0][index, rows, :] = high
    scatters[1][index, rows, :] = value - high


def left_dot(columns_ref, scatters, begin, width):
    high, low = [
        jnp.concatenate([part[begin + index].astype(jnp.bfloat16) for index in range(width)], 1) for part in scatters]
    return dot(columns_ref[3], high) + (dot(columns_ref[2], high) + dot(columns_ref[2], low))


def momentum_update(momentum, grads, taken, offsets, columns, band_rows, width):
    row_blocks, col_blocks = offsets.shape
    block_len = columns.shape[-1]
    span = width * block_len

    def kernel(offsets_ref, momentum_ref, grads_ref, taken_ref, columns_ref, out_ref, *scatters):
        for part in scatters:
            part[...] = jnp.zeros_like(part)
        for row in range(row_blocks):
            for chunk in range(col_blocks // width):
                base = row * col_blocks + chunk * width
                for index in range(width):
                    rows = pl.ds(offsets_ref[row, chunk * width + index], band_rows)
                    begin = (base + index) * band_rows
                    place_rows(scatters, base + index, rows, taken_ref[begin:begin + band_rows, :])
                inverse = left_dot(columns_ref, scatters, base, width)
                tile = (slice(row * block_len, (row + 1) * block_len), slice(chunk * span, (chunk + 1) * span))
                blended = momentum_decay * momentum_ref[tile].astype(jnp.float32) + grads_ref[(0,) + tile].astype(jnp.float32)
                blended = momentum_decay * blended + grads_ref[(1,) + tile].astype(jnp.float32)
                out_ref[tile] = (blended - inverse).astype(out_ref.dtype)

    return pl.pallas_call(
        kernel,
        in_specs=[SMEM] + [VMEM] * 4,
        out_specs=VMEM,
        out_shape=pltpu.VMEM(momentum.shape, momentum.dtype),
        scratch_shapes=[pltpu.VMEM((row_blocks * col_blocks, block_len, block_len), jnp.float32)] * 2,
        compiler_params=SMALL,
        name="momentum_update",
    )(offsets, *map(near_memory, (momentum, grads, taken, columns)))


def adam(kept, got, exp_avg, exp_sq, replicas, step_index):
    flat = exp_avg.shape
    block_len = flat[-1]

    def kernel(kept_ref, got_ref, avg_ref, sq_ref, avg_out, sq_out, raw_out, power_out):
        mean_band = (kept_ref[...] + got_ref[...].astype(jnp.float32)) / replicas
        avg = beta_one * avg_ref[...] + (1.0 - beta_one) * mean_band
        sq = beta_two * sq_ref[...] + (1.0 - beta_two) * mean_band * mean_band
        raw = avg / (jnp.sqrt(sq) + adam_eps)
        avg_out[...] = avg
        sq_out[...] = sq
        raw_out[...] = raw.astype(jnp.bfloat16)
        power_out[...] = jnp.sum((raw * raw).reshape(-1, 8, block_len), axis=0)

    return pl.pallas_call(
        kernel,
        in_specs=[VMEM] * 4,
        out_specs=[VMEM] * 4,
        out_shape=[pltpu.VMEM(flat, jnp.float32), pltpu.VMEM(flat, jnp.float32), pltpu.VMEM(flat, jnp.bfloat16),
                   pltpu.VMEM((8, block_len), jnp.float32)],
        compiler_params=SMALL,
        name=f"adam_{step_index}",
    )(*map(near_memory, (kept, got, exp_avg, exp_sq)))


def weights_update(weights, nears, fars, power, count_all, offsets, owners, columns, ready, orders, width):
    row_blocks, col_blocks = offsets.shape
    block_len = columns.shape[-1]
    half, band_rows, _ = nears[0].shape
    owned = col_blocks >> len(orders[0])
    slots = row_blocks * col_blocks
    chunks = col_blocks // width
    span = width * block_len
    count = len(ready)

    def kernel(offsets_ref, owners_ref, power_ref, weights_ref, columns_ref, *refs):
        near_refs, far_refs, ready_refs = refs[:STEPS], refs[STEPS:2 * STEPS], refs[2 * STEPS:2 * STEPS + count]
        refs = refs[2 * STEPS + count:]
        out_hbm, scales_ref, ready_hbm = refs[0], refs[1], refs[2:2 + count]
        out_ref, updates, departures, leaving, *scatters = refs[2 + count:]
        device = lax.axis_index("wide")
        copies = [
            pltpu.make_async_copy(source, target, leaving.at[index])
            for index, (source, target) in enumerate(zip(ready_refs, ready_hbm))
        ]
        for copy in copies:
            copy.start()
        for part in scatters:
            part[...] = jnp.zeros_like(part)
        scales = [jnp.sqrt(jnp.sum(power_ref[step_index], keepdims=True) / count_all + rms_eps) for step_index in range(STEPS)]
        for step_index in range(STEPS):
            scales_ref[step_index:step_index + 1, :] = jnp.broadcast_to(scales[step_index], (1, block_len))
        factors = [jnp.broadcast_to(1.0 / scale, (band_rows, block_len)) for scale in scales]
        for row in range(row_blocks):
            for chunk in range(chunks):
                base = row * col_blocks + chunk * width
                for index in range(width):
                    slot = owners_ref[row, chunk * width + index]
                    total = jnp.zeros((band_rows, block_len), jnp.float32)
                    for step_index, order in enumerate(orders):
                        place = slot_place(slot, device, order, row, row_blocks, owned)
                        is_near = place < half
                        entry = jnp.where(is_near, place, place - half)
                        raw = jnp.where(is_near, near_refs[step_index][entry], far_refs[step_index][entry])
                        total = total + raw.astype(jnp.float32) * factors[step_index]
                    begin = (base + index) * band_rows
                    updates[begin:begin + band_rows, :] = total
                begin = base * band_rows
                right = right_dot(updates[begin:begin + width * band_rows, :], columns_ref[0], columns_ref[1])
                for index in range(width):
                    rows = pl.ds(offsets_ref[row, chunk * width + index], band_rows)
                    place_rows(scatters, base + index, rows, right[index * band_rows:(index + 1) * band_rows])
                inverse = left_dot(columns_ref, scatters, base, width)
                tile = (slice(row * block_len, (row + 1) * block_len), slice(chunk * span, (chunk + 1) * span))
                out_ref[tile] = (weights_ref[tile].astype(jnp.float32) - learning_rate * inverse).astype(out_ref.dtype)
                copies.append(pltpu.make_async_copy(out_ref.at[tile], out_hbm.at[tile], departures.at[row, chunk]))
                copies[-1].start()
        for copy in copies:
            copy.wait()

    return pl.pallas_call(
        kernel,
        in_specs=[SMEM, SMEM] + [VMEM] * (3 + 2 * STEPS + count),
        out_specs=[HBM, VMEM] + [HBM] * count,
        out_shape=[
            pltpu.HBM(weights.shape, weights.dtype),
            pltpu.VMEM((STEPS, block_len), jnp.float32),
        ] + [pltpu.HBM(value.shape, value.dtype) for value in ready],
        scratch_shapes=[
            pltpu.VMEM(weights.shape, weights.dtype),
            pltpu.VMEM((slots * band_rows, block_len), jnp.float32),
            pltpu.SemaphoreType.DMA((row_blocks, chunks)),
            pltpu.SemaphoreType.DMA((count,)),
        ] + [pltpu.VMEM((slots, block_len, block_len), jnp.float32)] * 2,
        compiler_params=SMALL,
        name="weights_update",
    )(offsets, owners, *map(near_memory, (power, weights, columns, *nears, *fars, *ready)))


def swap(value, mask, replicas):
    return lax.ppermute(value, "wide", [(index, index ^ mask) for index in range(replicas)])


def across(value, mask, shift, replicas, shards):
    pairs = [(w * shards + s, (w ^ mask) * shards + (s ^ shift)) for w in range(replicas) for s in range(shards)]
    return lax.ppermute(value, ("wide", "shard"), pairs)


def tree_sum(values):
    while len(values) > 1:
        values = [a + b for a, b in zip(values[::2], values[1::2])]
    return values[0]


def per_device(weights, momentum, grads, offsets, owners, exp_avg, exp_sq):
    row_blocks, owned, band_rows, block_len = exp_avg.shape
    replicas = lax.axis_size("wide")
    shards = lax.axis_size("shard")
    count_all = exp_avg.size * replicas * shards
    table = dct_table(block_len)
    picks = jnp.asarray(row_tables(table))
    columns = jnp.asarray(column_tables(table))
    width = 16
    bits = replicas.bit_length() - 1
    orders = [list(range(bits)) for _ in range(STEPS)]
    if bits > 2:
        orders[1][1:3] = orders[1][2:0:-1]
    near_momentum, near_grads, taken, *rest = bands(
        momentum[0], grads[:, 0], offsets, owners, picks, columns, band_rows, orders, width)
    kept = rest[:STEPS]
    sent = rest[STEPS:]
    new_momentum = momentum_update(near_momentum, near_grads, taken, offsets, columns, band_rows, width)
    middle = kept[0].shape[0] - 1
    for stage in range(bits):
        got = []
        for step_index in range(STEPS):
            with jax.named_scope(f"scatter_{step_index}_{stage}"):
                got.append(swap(sent[step_index], 1 << orders[step_index][stage], replicas))
        if stage == bits - 1:
            break
        sums = [a[:middle] + b[:middle].astype(jnp.float32) for a, b in zip(kept, got)]
        middle //= 2
        kept = [value[:middle] for value in sums]
        sent = [value[middle:].astype(jnp.bfloat16) for value in sums]
    avg_now = exp_avg.reshape(row_blocks * owned, band_rows, block_len)
    sq_now = exp_sq.reshape(row_blocks * owned, band_rows, block_len)
    nears = []
    powers = []
    for step_index in range(STEPS):
        avg_now, sq_now, raw, power = adam(kept[step_index], got[step_index], avg_now, sq_now, replicas, step_index)
        nears.append(raw)
        powers.append(power)
    power = jnp.stack(powers)
    for stage in reversed(range(bits)):
        fars = []
        for step_index in range(STEPS):
            with jax.named_scope(f"gather_{step_index}_{stage}"):
                fars.append(swap(nears[step_index], 1 << orders[step_index][stage], replicas))
        mask = 1 << orders[-1][stage]
        with jax.named_scope(f"power_{stage}"):
            if stage == bits - 1:
                others = [across(power, flip, shift, replicas, shards) for flip in (0, mask) for shift in range(shards)
                          if flip or shift]
            else:
                others = [swap(power, mask, replicas)]
        fars[-1], others = lax.optimization_barrier((fars[-1], others))
        power = tree_sum([power] + others)
        if stage > 0:
            nears = [jnp.concatenate([near, far], 0) for near, far in zip(nears, fars)]
    new_weights, scales, new_momentum, avg_now, sq_now = weights_update(
        weights, nears, fars, power, count_all, offsets, owners, columns, (new_momentum, avg_now, sq_now), orders, width)
    return (new_weights, new_momentum[None], avg_now.reshape(exp_avg.shape), sq_now.reshape(exp_sq.shape), scales[:, 0])


def solution(mesh):
    in_specs = (
        P("shard", None),
        P("wide", "shard", None),
        P(None, "wide", "shard", None),
        P("shard", None),
        P("shard", None),
        P("shard", "wide", None, None),
        P("shard", "wide", None, None),
    )
    out_specs = (
        P("shard", None),
        P("wide", "shard", None),
        P("shard", "wide", None, None),
        P("shard", "wide", None, None),
        P(),
    )
    return jax.shard_map(
        per_device, mesh=mesh, in_specs=in_specs, out_specs=out_specs, check_vma=False
    )
```

```python
import jax
import jax.numpy as jnp
import numpy as np
from jax import lax
from jax.experimental import pallas as pl
from jax.experimental.pallas import tpu as pltpu
from jax.sharding import PartitionSpec as P


STEPS = 2

momentum_decay = 0.9
beta_one = 0.8
beta_two = 0.95
adam_eps = 1e-08
rms_eps = 1e-06
learning_rate = 0.2


SMEM = pl.BlockSpec(memory_space=pltpu.SMEM)
VMEM = pl.BlockSpec(memory_space=pltpu.VMEM)
ANY = pl.BlockSpec(memory_space=pl.ANY)
HBM = pl.BlockSpec(memory_space=pltpu.HBM)
SMALL = pltpu.CompilerParams(vmem_limit_bytes=20 << 20)


def dct_table(length):
    frequency = np.arange(length, dtype=np.float64)[:, None]
    position = np.arange(length, dtype=np.float64)[None, :]
    cosines = np.cos(np.pi * (2.0 * position + 1.0) * frequency / (2.0 * length))
    scaling = np.where(frequency == 0.0, np.sqrt(1.0 / length), np.sqrt(2.0 / length))
    return (cosines * scaling).astype(np.float32)


def split_table(table):
    high = table.astype(jnp.bfloat16)
    low = (table - high.astype(np.float32)).astype(jnp.bfloat16)
    return high, low


def row_tables(table):
    high, low = split_table(table)
    decayed_high, decayed_low = split_table(np.float32(momentum_decay) * table)
    wide = table.astype(np.float64)
    residue = momentum_decay * (np.eye(len(table)) - wide @ wide.T)
    parts = (high, low, decayed_high, decayed_low, residue.astype(np.float32).astype(jnp.bfloat16))
    return np.stack([part.astype(np.float32) for part in parts])


def column_tables(table):
    high, low = split_table(table)
    zero = np.zeros_like(low)
    rights = [np.block([[h, l], [h, zero]]) for h, l in ((high, low), (high.T, low.T))]
    lefts = np.block([[high.T, high.T], [low.T, zero]])
    return np.stack([*rights, lefts])


def near_memory(value):
    return pltpu.with_memory_space_constraint(value, pltpu.VMEM)


def far_memory(value):
    return pltpu.with_memory_space_constraint(value, pltpu.HBM)


def halves(value):
    high = value.astype(jnp.bfloat16)
    return high, (value - high.astype(jnp.float32)).astype(jnp.bfloat16)


def dot(left, right):
    return jnp.dot(left, right, preferred_element_type=jnp.float32)


def right_dot(left, table):
    length = left.shape[1]
    both = dot(jnp.concatenate(halves(left), 1), table)
    return both[:, :length] + both[:, length:]


def block_of(part, chunks, row_blocks):
    return (0, part) if row_blocks == 1 else (part // chunks, part % chunks)


def fill_groups(groups_ref, orders):
    for role, order in enumerate(orders):
        for relative in range(1 << len(order)):
            place = 0
            for bit in order:
                place = place * 2 + ((relative >> bit) & 1)
            groups_ref[role, relative] = place


def slot_places(groups_ref, slot, device, row, row_blocks, owned):
    if owned & (owned - 1) == 0:
        relative = (slot >> (owned.bit_length() - 1)) ^ device
        within = slot & (owned - 1)
    else:
        relative = lax.div(slot, owned) ^ device
        within = lax.rem(slot, owned)
    role = device & 1
    within = row * owned + within
    size = row_blocks * owned
    return groups_ref[role, relative] * size + within, groups_ref[1 - role, relative ^ 1] * size + within


def bands(momentum, grads, offsets, owners, picks, columns, band_rows, orders, width):
    row_blocks, col_blocks = offsets.shape
    block_len = picks.shape[-1]
    owned = col_blocks >> len(orders[0])
    slots = row_blocks * col_blocks
    chunks = col_blocks // width
    span = width * block_len

    def kernel(offsets_hbm, owners_hbm, momentum_hbm, grads_hbm, picks_hbm, columns_hbm, momentum_ref, grads_ref, taken_ref,
               keep_ref, send_ref, offsets_ref, owners_ref, groups_ref, picks_ref, columns_ref, lefts, tables, arrivals, *scatters):
        device = lax.axis_index("wide")
        first_role = (device & 1) == 0
        small = [
            pltpu.make_async_copy(source, target, tables.at[index])
            for index, (source, target) in enumerate([
                (offsets_hbm, offsets_ref), (owners_hbm, owners_ref), (picks_hbm, picks_ref), (columns_hbm, columns_ref)])
        ]
        for copy in small:
            copy.start()

        def arrival(part):
            row, chunk = block_of(part, chunks, row_blocks)
            rows = pl.ds(row * block_len, block_len)
            lanes = pl.ds(chunk * span, span)
            return [
                pltpu.make_async_copy(momentum_hbm.at[rows, lanes], momentum_ref.at[rows, lanes], arrivals.at[0, part]),
                pltpu.make_async_copy(grads_hbm.at[:, rows, lanes], grads_ref.at[:, rows, lanes], arrivals.at[1, part]),
            ]

        for part in range(row_blocks * chunks):
            for copy in arrival(part):
                copy.start()
        fill_groups(groups_ref, orders)
        blank = jnp.zeros((band_rows, block_len), jnp.float32)
        for scatter in scatters:
            scatter[...] = jnp.zeros_like(scatter)
        for copy in small:
            copy.wait()

        def body(part, carry):
            for copy in arrival(part):
                copy.wait()
            row, chunk = block_of(part, chunks, row_blocks)
            block_rows = slice(0, block_len) if row_blocks == 1 else pl.ds(pl.multiple_of(row * block_len, block_len), block_len)
            taken_start = part * width * band_rows
            ranges = [pl.ds(offsets_ref[row, chunk * width + index], band_rows) for index in range(width)]
            columns_of = [
                pl.ds(pl.multiple_of((chunk * width + index) * block_len, block_len), block_len) for index in range(width)]
            for index, (rows, lanes) in enumerate(zip(ranges, columns_of)):
                high, low, decayed_high, decayed_low = [picks_ref[number, rows, :].astype(jnp.bfloat16) for number in range(4)]
                first = jnp.concatenate(
                    [jnp.concatenate([decayed_high, high], 1), jnp.concatenate([decayed_low, low], 1)], 0)
                pair = dot(first, jnp.concatenate([momentum_ref[block_rows, lanes], grads_ref[0, block_rows, lanes]], 0))
                left = pair[:band_rows] + pair[band_rows:]
                scatters[index][rows, :] = left
                lefts[index * band_rows:(index + 1) * band_rows, :] = left
            for index, (rows, lanes) in enumerate(zip(ranges, columns_of)):
                high, low, residue = [picks_ref[number, rows, :].astype(jnp.bfloat16) for number in (0, 1, 4)]
                second = jnp.concatenate(
                    [jnp.concatenate([high, residue], 1), jnp.concatenate([low, jnp.zeros_like(low)], 1)], 0)
                pair = dot(second, jnp.concatenate(
                    [grads_ref[1, block_rows, lanes], scatters[index][...].astype(jnp.bfloat16)], 0))
                scatters[index][rows, :] = blank
                left = pair[:band_rows] + pair[band_rows:]
                lefts[(width + index) * band_rows:(width + index + 1) * band_rows, :] = left
                taken_ref[pl.ds(pl.multiple_of(taken_start + index * band_rows, band_rows), band_rows), :] = (
                    momentum_decay * lefts[index * band_rows:(index + 1) * band_rows, :] + left)
            band = right_dot(lefts[...], columns_ref[1])
            for index in range(width):
                slot = owners_ref[row, chunk * width + index]
                here, there = slot_places(groups_ref, slot, device, row, row_blocks, owned)
                values = [band[(step_index * width + index) * band_rows:(step_index * width + index + 1) * band_rows]
                          for step_index in range(STEPS)]
                keep_ref[here] = jnp.where(first_role, values[0], values[1])
                send_ref[there] = jnp.where(first_role, values[1], values[0]).astype(jnp.bfloat16)
            return carry

        lax.fori_loop(0, row_blocks * chunks, body, 0)

    shape = (slots, band_rows, block_len)
    return pl.pallas_call(
        kernel,
        in_specs=[HBM] * 6,
        out_specs=[VMEM] * 5,
        out_shape=[
            pltpu.VMEM(momentum.shape, momentum.dtype),
            pltpu.VMEM(grads.shape, grads.dtype),
            pltpu.VMEM((slots * band_rows, block_len), jnp.float32),
            pltpu.VMEM(shape, jnp.float32),
            pltpu.VMEM(shape, jnp.bfloat16),
        ],
        scratch_shapes=[
            pltpu.SMEM(offsets.shape, offsets.dtype),
            pltpu.SMEM(owners.shape, owners.dtype),
            pltpu.SMEM((STEPS, 1 << len(orders[0])), jnp.int32),
            pltpu.VMEM(picks.shape, picks.dtype),
            pltpu.VMEM(columns.shape, columns.dtype),
            pltpu.VMEM((STEPS * width * band_rows, block_len), jnp.float32),
            pltpu.SemaphoreType.DMA((4,)),
            pltpu.SemaphoreType.DMA((2, row_blocks * chunks)),
        ] + [pltpu.VMEM((block_len, block_len), jnp.float32)] * width,
        compiler_params=SMALL,
        name="bands",
    )(*map(far_memory, (offsets, owners, momentum, grads, picks, columns)))


def left_dot(columns_ref, scatters, ranges, values):
    blank = jnp.zeros_like(values[0])
    highs = []
    lows = []
    for (high_ref, low_ref), rows, value in zip(scatters, ranges, values):
        high = value.astype(jnp.bfloat16).astype(jnp.float32)
        high_ref[rows, :] = high
        low_ref[rows, :] = value - high
        highs.append(high_ref[...].astype(jnp.bfloat16))
        lows.append(low_ref[...].astype(jnp.bfloat16))
        high_ref[rows, :] = blank
        low_ref[rows, :] = blank
    high = jnp.concatenate(highs, 1)
    low = jnp.concatenate(lows, 1)
    length = high.shape[0]
    return dot(columns_ref[2, :length], jnp.concatenate([high, low], 0)) + dot(columns_ref[2, length:, :length], high)


def clear(scatters):
    for part in scatters:
        part[...] = jnp.zeros_like(part)
    return list(zip(scatters[::2], scatters[1::2]))


def momentum_update(momentum, grads, taken, offsets, columns, band_rows, width):
    row_blocks, col_blocks = offsets.shape
    block_len = columns.shape[-1] // 2
    chunks = col_blocks // width
    span = width * block_len

    def kernel(offsets_ref, momentum_ref, grads_ref, taken_ref, columns_ref, out_ref, *scatters):
        scatters = clear(scatters)

        def body(part, carry):
            row, chunk = block_of(part, chunks, row_blocks)
            ranges = [pl.ds(offsets_ref[row, chunk * width + index], band_rows) for index in range(width)]
            values = [
                taken_ref[pl.ds(pl.multiple_of((part * width + index) * band_rows, band_rows), band_rows), :]
                for index in range(width)]
            inverse = left_dot(columns_ref, scatters, ranges, values)
            tile = (pl.ds(pl.multiple_of(row * block_len, block_len), block_len),
                    pl.ds(pl.multiple_of(chunk * span, span), span))
            blended = momentum_decay * momentum_ref[tile].astype(jnp.float32) + grads_ref[(0,) + tile].astype(jnp.float32)
            blended = momentum_decay * blended + grads_ref[(1,) + tile].astype(jnp.float32)
            out_ref[tile] = (blended - inverse).astype(out_ref.dtype)
            return carry

        lax.fori_loop(0, row_blocks * chunks, body, 0)

    return pl.pallas_call(
        kernel,
        in_specs=[SMEM] + [VMEM] * 4,
        out_specs=VMEM,
        out_shape=pltpu.VMEM(momentum.shape, momentum.dtype),
        scratch_shapes=[pltpu.VMEM((block_len, block_len), jnp.float32)] * (2 * width),
        compiler_params=SMALL,
        name="momentum_update",
    )(offsets, *map(near_memory, (momentum, grads, taken, columns)))


def adam(mine, got, exp_avg, exp_sq, replicas):
    flat = exp_avg.shape
    block_len = flat[-1]

    def kernel(mine_ref, got_ref, avg_ref, sq_ref, avg_out, sq_out, raw_keep, raw_send, power_keep, power_send):
        first_role = (lax.axis_index("wide") & 1) == 0
        own = mine_ref[...]
        other = got_ref[...]
        avg = avg_ref[...]
        sq = sq_ref[...]
        raws = []
        powers = []
        for total in (jnp.where(first_role, own, other), jnp.where(first_role, other, own)):
            mean_band = total / replicas
            avg = beta_one * avg + (1.0 - beta_one) * mean_band
            sq = beta_two * sq + (1.0 - beta_two) * mean_band * mean_band
            raw = avg / (jnp.sqrt(sq) + adam_eps)
            raws.append(raw)
            powers.append(jnp.sum((raw * raw).reshape(-1, 8, block_len), axis=0))
        avg_out[...] = avg
        sq_out[...] = sq
        raw_keep[...] = jnp.where(first_role, raws[0], raws[1]).astype(jnp.bfloat16)
        raw_send[...] = jnp.where(first_role, raws[1], raws[0]).astype(jnp.bfloat16)
        power_keep[...] = jnp.where(first_role, powers[0], powers[1])
        power_send[...] = jnp.where(first_role, powers[1], powers[0])

    return pl.pallas_call(
        kernel,
        in_specs=[VMEM] * 4,
        out_specs=[VMEM] * 6,
        out_shape=[pltpu.VMEM(flat, jnp.float32)] * 2 + [pltpu.VMEM(flat, jnp.bfloat16)] * 2
        + [pltpu.VMEM((8, block_len), jnp.float32)] * 2,
        compiler_params=SMALL,
        name="adam",
    )(*map(near_memory, (mine, got, exp_avg, exp_sq)))


def weights_update(weights, pieces, powers, count_all, offsets, owners, columns, ready, orders, width):
    row_blocks, col_blocks = offsets.shape
    block_len = columns.shape[-1] // 2
    half, band_rows, _ = pieces[0].shape
    owned = col_blocks >> len(orders[0])
    chunks = col_blocks // width
    span = width * block_len
    count = len(ready)

    def kernel(offsets_ref, owners_ref, own_power, other_power, weights_ref, columns_ref, *refs):
        piece_refs, ready_refs = refs[:2 * STEPS], refs[2 * STEPS:2 * STEPS + count]
        refs = refs[2 * STEPS + count:]
        out_hbm, scales_ref, ready_hbm = refs[0], refs[1], refs[2:2 + count]
        groups_ref, out_ref, departures, leaving, *scatters = refs[2 + count:]
        device = lax.axis_index("wide")
        first_role = (device & 1) == 0
        copies = [
            pltpu.make_async_copy(source, target, leaving.at[index])
            for index, (source, target) in enumerate(zip(ready_refs, ready_hbm))
        ]
        for copy in copies:
            copy.start()
        fill_groups(groups_ref, orders)
        scatters = clear(scatters)
        scales = [
            jnp.broadcast_to(jnp.sqrt(jnp.sum(power[...], keepdims=True) / count_all + rms_eps), (1, block_len))
            for power in (own_power, other_power)]
        scales_ref[0] = jnp.where(first_role, scales[0], scales[1])[0, 0]
        scales_ref[1] = jnp.where(first_role, scales[1], scales[0])[0, 0]
        factors = [jnp.broadcast_to(1.0 / scale, (band_rows, block_len)) for scale in scales]

        def tile_of(part):
            row, chunk = block_of(part, chunks, row_blocks)
            return (pl.ds(pl.multiple_of(row * block_len, block_len), block_len),
                    pl.ds(pl.multiple_of(chunk * span, span), span))

        def departure(part):
            tile = tile_of(part)
            return pltpu.make_async_copy(out_ref.at[tile], out_hbm.at[tile], departures.at[part])

        def body(part, carry):
            row, chunk = block_of(part, chunks, row_blocks)
            totals = []
            for index in range(width):
                slot = owners_ref[row, chunk * width + index]
                places = slot_places(groups_ref, slot, device, row, row_blocks, owned)
                total = jnp.zeros((band_rows, block_len), jnp.float32)
                for number, place in enumerate(places):
                    is_near = place < half
                    entry = jnp.where(is_near, place, place - half)
                    raw = jnp.where(is_near, piece_refs[2 * number][entry], piece_refs[2 * number + 1][entry])
                    total = total + raw.astype(jnp.float32) * factors[number]
                totals.append(total)
            right = right_dot(jnp.concatenate(totals, 0), columns_ref[0])
            ranges = [pl.ds(offsets_ref[row, chunk * width + index], band_rows) for index in range(width)]
            values = [right[index * band_rows:(index + 1) * band_rows] for index in range(width)]
            inverse = left_dot(columns_ref, scatters, ranges, values)
            tile = tile_of(part)
            out_ref[tile] = (weights_ref[tile].astype(jnp.float32) - learning_rate * inverse).astype(out_ref.dtype)
            departure(part).start()
            return carry

        lax.fori_loop(0, row_blocks * chunks, body, 0)
        for part in range(row_blocks * chunks):
            departure(part).wait()
        for copy in copies:
            copy.wait()

    return pl.pallas_call(
        kernel,
        in_specs=[SMEM, SMEM] + [VMEM] * (4 + 2 * STEPS + count),
        out_specs=[HBM, SMEM] + [HBM] * count,
        out_shape=[
            pltpu.HBM(weights.shape, weights.dtype),
            jax.ShapeDtypeStruct((STEPS,), jnp.float32),
        ] + [pltpu.HBM(value.shape, value.dtype) for value in ready],
        scratch_shapes=[
            pltpu.SMEM((STEPS, 1 << len(orders[0])), jnp.int32),
            pltpu.VMEM(weights.shape, weights.dtype),
            pltpu.SemaphoreType.DMA((row_blocks * chunks,)),
            pltpu.SemaphoreType.DMA((count,)),
        ] + [pltpu.VMEM((block_len, block_len), jnp.float32)] * (2 * width),
        compiler_params=SMALL,
        name="weights_update",
    )(offsets, owners, *map(near_memory, (*powers, weights, columns, *pieces, *ready)))


def swap(value, orders, stage):
    pairs = [(index, index ^ (1 << orders[index & 1][stage])) for index in range(1 << len(orders[0]))]
    return lax.ppermute(value, "wide", pairs)


def across(value, orders, stage, shift, shards):
    pairs = []
    for index in range(1 << len(orders[0])):
        partner = index if stage is None else index ^ (1 << orders[index & 1][stage])
        pairs += [(index * shards + shard, partner * shards + (shard ^ shift)) for shard in range(shards)]
    return lax.ppermute(value, ("wide", "shard"), pairs)


def tree_sum(values):
    while len(values) > 1:
        values = [a + b for a, b in zip(values[::2], values[1::2])]
    return values[0]


def per_device(weights, momentum, grads, offsets, owners, exp_avg, exp_sq):
    row_blocks, owned, band_rows, block_len = exp_avg.shape
    replicas = lax.axis_size("wide")
    shards = lax.axis_size("shard")
    count_all = exp_avg.size * replicas * shards
    table = dct_table(block_len)
    picks = jnp.asarray(row_tables(table))
    columns = jnp.asarray(column_tables(table))
    width = 16
    bits = replicas.bit_length() - 1
    orders = [list(range(1, bits)) + [0] for _ in range(STEPS)]
    if bits > 3:
        orders[1][:2] = orders[1][1::-1]
    core = bits - 1
    near_momentum, near_grads, taken, kept, sent = bands(
        momentum[0], grads[:, 0], offsets, owners, picks, columns, band_rows, orders, width)
    new_momentum = momentum_update(near_momentum, near_grads, taken, offsets, columns, band_rows, width)
    got = swap(sent, orders, core)
    kept = kept + got.astype(jnp.float32)
    for stage in range(core):
        middle = kept.shape[0] // 2
        got = swap(kept[middle:].astype(jnp.bfloat16), orders, stage)
        kept = kept[:middle] + got.astype(jnp.float32)
    middle = kept.shape[0] // 2
    got = swap(kept[middle:], orders, core)
    flat = (row_blocks * owned, band_rows, block_len)
    avg_now, sq_now, raw, raw_other, power, power_other = adam(
        kept[:middle], got, exp_avg.reshape(flat), exp_sq.reshape(flat), replicas)
    far = swap(raw_other, orders, core)
    power_far = swap(power_other, orders, core)
    near = jnp.concatenate([raw, far], 0)
    power = power + power_far
    for stage in reversed(range(core)):
        far = swap(near, orders, stage)
        others = [swap(power, orders, stage)]
        if stage == core - 1:
            for shift in range(1, shards):
                others += [across(power, orders, None, shift, shards), across(power, orders, stage, shift, shards)]
        far, others = lax.optimization_barrier((far, others))
        power = tree_sum([power] + others)
        if stage > 0:
            near = jnp.concatenate([near, far], 0)
    pieces = [near, far, swap(near, orders, core), swap(far, orders, core)]
    powers = [power, swap(power, orders, core)]
    new_weights, scales, new_momentum, avg_now, sq_now = weights_update(
        weights, pieces, powers, count_all, offsets, owners, columns, (new_momentum, avg_now, sq_now), orders, width)
    return (new_weights, new_momentum[None], avg_now.reshape(exp_avg.shape), sq_now.reshape(exp_sq.shape), scales)


def solution(mesh):
    in_specs = (
        P("shard", None),
        P("wide", "shard", None),
        P(None, "wide", "shard", None),
        P("shard", None),
        P("shard", None),
        P("shard", "wide", None, None),
        P("shard", "wide", None, None),
    )
    out_specs = (
        P("shard", None),
        P("wide", "shard", None),
        P("shard", "wide", None, None),
        P("shard", "wide", None, None),
        P(),
    )
    return jax.shard_map(per_device, mesh=mesh, in_specs=in_specs, out_specs=out_specs, check_vma=False)
```

```python
import jax
import jax.numpy as jnp
import numpy as np
from jax import lax
from jax.experimental import pallas as pl
from jax.experimental.pallas import tpu as pltpu
from jax.sharding import PartitionSpec as P


STEPS = 2
TILE = 16

momentum_decay = 0.9
beta_one = 0.8
beta_two = 0.95
adam_eps = 1e-08
rms_eps = 1e-06
learning_rate = 0.2


SMEM = pl.BlockSpec(memory_space=pltpu.SMEM)
VMEM = pl.BlockSpec(memory_space=pltpu.VMEM)
ANY = pl.BlockSpec(memory_space=pl.ANY)
HBM = pl.BlockSpec(memory_space=pltpu.HBM)
SMALL = pltpu.CompilerParams(vmem_limit_bytes=20 << 20)


def dct_table(length):
    frequency = np.arange(length, dtype=np.float64)[:, None]
    position = np.arange(length, dtype=np.float64)[None, :]
    cosines = np.cos(np.pi * (2.0 * position + 1.0) * frequency / (2.0 * length))
    scaling = np.where(frequency == 0.0, np.sqrt(1.0 / length), np.sqrt(2.0 / length))
    return (cosines * scaling).astype(np.float32)


def split_table(table):
    high = table.astype(jnp.bfloat16)
    low = (table - high.astype(np.float32)).astype(jnp.bfloat16)
    return high, low


def row_tables(table):
    high, low = split_table(table)
    decayed_high, decayed_low = split_table(np.float32(momentum_decay) * table)
    wide = table.astype(np.float64)
    residue = momentum_decay * (np.eye(len(table)) - wide @ wide.T)
    parts = (high, low, decayed_high, decayed_low, residue.astype(np.float32).astype(jnp.bfloat16))
    return np.stack([part.astype(np.float32) for part in parts])


def column_tables(table):
    high, low = split_table(table)
    zero = np.zeros_like(low)
    rights = [np.block([[h, l], [h, zero]]) for h, l in ((high, low), (high.T, low.T))]
    lefts = np.block([[high.T, high.T], [low.T, zero]])
    return np.stack([*rights, lefts])


def near_memory(value):
    return pltpu.with_memory_space_constraint(value, pltpu.VMEM)


def far_memory(value):
    return pltpu.with_memory_space_constraint(value, pltpu.HBM)


def halves(value):
    high = value.astype(jnp.bfloat16)
    return high, (value - high.astype(jnp.float32)).astype(jnp.bfloat16)


def dot(left, right):
    return jnp.dot(left, right, preferred_element_type=jnp.float32)


def right_dot(left, table):
    length = left.shape[1]
    both = dot(jnp.concatenate(halves(left), 1), table)
    return both[:, :length] + both[:, length:]


def block_of(part, chunks, row_blocks):
    return (0, part) if row_blocks == 1 else (part // chunks, part % chunks)


def fill_groups(groups_ref, orders):
    for role, order in enumerate(orders):
        for relative in range(1 << len(order)):
            place = 0
            for bit in order:
                place = place * 2 + ((relative >> bit) & 1)
            groups_ref[role, relative] = place


def owner_of(slot, owned):
    if owned & (owned - 1) == 0:
        return slot >> (owned.bit_length() - 1), slot & (owned - 1)
    return lax.div(slot, owned), lax.rem(slot, owned)


def slot_places(groups_ref, slot, device, row, owned, size):
    owner, within = owner_of(slot, owned)
    relative = owner ^ device
    role = device & 1
    within = row * owned + within
    return groups_ref[role, relative] * size + within, groups_ref[1 - role, relative ^ 1] * size + within


def bands(momentum, grads, offsets, owners, picks, columns, band_rows, orders, width):
    row_blocks, col_blocks = offsets.shape
    block_len = picks.shape[-1]
    owned = col_blocks >> len(orders[0])
    slots = row_blocks * col_blocks
    chunks = col_blocks // width
    span = width * block_len

    def kernel(offsets_hbm, owners_hbm, momentum_hbm, grads_hbm, picks_hbm, columns_hbm, momentum_ref, grads_ref, taken_ref,
               keep_ref, send_ref, offsets_ref, owners_ref, groups_ref, picks_ref, columns_ref, lefts, tables, arrivals, *scatters):
        device = lax.axis_index("wide")
        first_role = (device & 1) == 0
        small = [
            pltpu.make_async_copy(source, target, tables.at[index])
            for index, (source, target) in enumerate([
                (offsets_hbm, offsets_ref), (owners_hbm, owners_ref), (picks_hbm, picks_ref), (columns_hbm, columns_ref)])
        ]
        for copy in small:
            copy.start()

        def arrival(part):
            row, chunk = block_of(part, chunks, row_blocks)
            rows = pl.ds(row * block_len, block_len)
            lanes = pl.ds(chunk * span, span)
            return [
                pltpu.make_async_copy(momentum_hbm.at[rows, lanes], momentum_ref.at[rows, lanes], arrivals.at[0, part]),
                pltpu.make_async_copy(grads_hbm.at[:, rows, lanes], grads_ref.at[:, rows, lanes], arrivals.at[1, part]),
            ]

        for part in range(row_blocks * chunks):
            for copy in arrival(part):
                copy.start()
        fill_groups(groups_ref, orders)
        blank = jnp.zeros((band_rows, block_len), jnp.float32)
        for scatter in scatters:
            scatter[...] = jnp.zeros_like(scatter)
        for copy in small:
            copy.wait()

        def body(part, carry):
            for copy in arrival(part):
                copy.wait()
            row, chunk = block_of(part, chunks, row_blocks)
            block_rows = slice(0, block_len) if row_blocks == 1 else pl.ds(pl.multiple_of(row * block_len, block_len), block_len)
            taken_start = part * width * band_rows
            ranges = [pl.ds(offsets_ref[row, chunk * width + index], band_rows) for index in range(width)]
            columns_of = [
                pl.ds(pl.multiple_of((chunk * width + index) * block_len, block_len), block_len) for index in range(width)]
            for index, (rows, lanes) in enumerate(zip(ranges, columns_of)):
                high, low, decayed_high, decayed_low = [picks_ref[number, rows, :].astype(jnp.bfloat16) for number in range(4)]
                first = jnp.concatenate(
                    [jnp.concatenate([decayed_high, high], 1), jnp.concatenate([decayed_low, low], 1)], 0)
                pair = dot(first, jnp.concatenate([momentum_ref[block_rows, lanes], grads_ref[0, block_rows, lanes]], 0))
                left = pair[:band_rows] + pair[band_rows:]
                scatters[index][rows, :] = left
                lefts[index * band_rows:(index + 1) * band_rows, :] = left
            for index, (rows, lanes) in enumerate(zip(ranges, columns_of)):
                high, low, residue = [picks_ref[number, rows, :].astype(jnp.bfloat16) for number in (0, 1, 4)]
                second = jnp.concatenate(
                    [jnp.concatenate([high, residue], 1), jnp.concatenate([low, jnp.zeros_like(low)], 1)], 0)
                pair = dot(second, jnp.concatenate(
                    [grads_ref[1, block_rows, lanes], scatters[index][...].astype(jnp.bfloat16)], 0))
                scatters[index][rows, :] = blank
                left = pair[:band_rows] + pair[band_rows:]
                lefts[(width + index) * band_rows:(width + index + 1) * band_rows, :] = left
                taken_ref[pl.ds(pl.multiple_of(taken_start + index * band_rows, band_rows), band_rows), :] = (
                    momentum_decay * lefts[index * band_rows:(index + 1) * band_rows, :] + left)
            band = right_dot(lefts[...], columns_ref[1])
            for index in range(width):
                slot = owners_ref[row, chunk * width + index]
                here, there = slot_places(groups_ref, slot, device, row, owned, row_blocks * owned)
                values = [band[(step_index * width + index) * band_rows:(step_index * width + index + 1) * band_rows]
                          for step_index in range(STEPS)]
                keep_ref[here] = jnp.where(first_role, values[0], values[1])
                send_ref[there] = jnp.where(first_role, values[1], values[0]).astype(jnp.bfloat16)
            return carry

        lax.fori_loop(0, row_blocks * chunks, body, 0)

    shape = (slots, band_rows, block_len)
    return pl.pallas_call(
        kernel,
        in_specs=[HBM] * 6,
        out_specs=[VMEM] * 5,
        out_shape=[
            pltpu.VMEM(momentum.shape, momentum.dtype),
            pltpu.VMEM(grads.shape, grads.dtype),
            pltpu.VMEM((slots * band_rows, block_len), jnp.float32),
            pltpu.VMEM(shape, jnp.float32),
            pltpu.VMEM(shape, jnp.bfloat16),
        ],
        scratch_shapes=[
            pltpu.SMEM(offsets.shape, offsets.dtype),
            pltpu.SMEM(owners.shape, owners.dtype),
            pltpu.SMEM((STEPS, 1 << len(orders[0])), jnp.int32),
            pltpu.VMEM(picks.shape, picks.dtype),
            pltpu.VMEM(columns.shape, columns.dtype),
            pltpu.VMEM((STEPS * width * band_rows, block_len), jnp.float32),
            pltpu.SemaphoreType.DMA((4,)),
            pltpu.SemaphoreType.DMA((2, row_blocks * chunks)),
        ] + [pltpu.VMEM((block_len, block_len), jnp.float32)] * width,
        compiler_params=SMALL,
        name="bands",
    )(*map(far_memory, (offsets, owners, momentum, grads, picks, columns)))


def left_dot(columns_ref, scatters, ranges, values):
    blank = jnp.zeros_like(values[0])
    highs = []
    lows = []
    for (high_ref, low_ref), rows, value in zip(scatters, ranges, values):
        high = value.astype(jnp.bfloat16).astype(jnp.float32)
        high_ref[rows, :] = high
        low_ref[rows, :] = value - high
        highs.append(high_ref[...].astype(jnp.bfloat16))
        lows.append(low_ref[...].astype(jnp.bfloat16))
        high_ref[rows, :] = blank
        low_ref[rows, :] = blank
    high = jnp.concatenate(highs, 1)
    low = jnp.concatenate(lows, 1)
    length = high.shape[0]
    return dot(columns_ref[2, :length], jnp.concatenate([high, low], 0)) + dot(columns_ref[2, length:, :length], high)


def clear(scatters):
    for part in scatters:
        part[...] = jnp.zeros_like(part)
    return list(zip(scatters[::2], scatters[1::2]))


def momentum_update(momentum, grads, taken, offsets, columns, band_rows, width):
    row_blocks, col_blocks = offsets.shape
    block_len = columns.shape[-1] // 2
    chunks = col_blocks // width
    span = width * block_len

    def kernel(offsets_ref, momentum_ref, grads_ref, taken_ref, columns_ref, out_ref, *scatters):
        scatters = clear(scatters)

        def body(part, carry):
            row, chunk = block_of(part, chunks, row_blocks)
            ranges = [pl.ds(offsets_ref[row, chunk * width + index], band_rows) for index in range(width)]
            values = [
                taken_ref[pl.ds(pl.multiple_of((part * width + index) * band_rows, band_rows), band_rows), :]
                for index in range(width)]
            inverse = left_dot(columns_ref, scatters, ranges, values)
            tile = (pl.ds(pl.multiple_of(row * block_len, block_len), block_len),
                    pl.ds(pl.multiple_of(chunk * span, span), span))
            blended = momentum_decay * momentum_ref[tile].astype(jnp.float32) + grads_ref[(0,) + tile].astype(jnp.float32)
            blended = momentum_decay * blended + grads_ref[(1,) + tile].astype(jnp.float32)
            out_ref[tile] = (blended - inverse).astype(out_ref.dtype)
            return carry

        lax.fori_loop(0, row_blocks * chunks, body, 0)

    return pl.pallas_call(
        kernel,
        in_specs=[SMEM] + [VMEM] * 4,
        out_specs=VMEM,
        out_shape=pltpu.VMEM(momentum.shape, momentum.dtype),
        scratch_shapes=[pltpu.VMEM((block_len, block_len), jnp.float32)] * (2 * width),
        compiler_params=SMALL,
        name="momentum_update",
    )(offsets, *map(near_memory, (momentum, grads, taken, columns)))


def adam(mine, got, exp_avg, exp_sq, replicas):
    flat = exp_avg.shape
    block_len = flat[-1]
    rows = flat[0] * flat[1]

    def kernel(mine_ref, got_ref, avg_ref, sq_ref, avg_out, sq_out, raw_keep, raw_send):
        first_role = (lax.axis_index("wide") & 1) == 0
        own = mine_ref[...]
        other = got_ref[...]
        avg = avg_ref[...]
        sq = sq_ref[...]
        row = lax.broadcasted_iota(jnp.int32, (TILE, block_len), 0)
        tile = jnp.zeros((TILE, block_len), jnp.float32)
        raws = []
        for step_index, total in enumerate((jnp.where(first_role, own, other), jnp.where(first_role, other, own))):
            mean_band = total / replicas
            avg = beta_one * avg + (1.0 - beta_one) * mean_band
            sq = beta_two * sq + (1.0 - beta_two) * mean_band * mean_band
            raw = avg / (jnp.sqrt(sq) + adam_eps)
            raws.append(raw.reshape(rows, block_len))
            rest = jnp.sum(raws[-1] * raws[-1], axis=0, keepdims=True)
            for part in range(3):
                piece = rest.astype(jnp.bfloat16).astype(jnp.float32)
                tile = jnp.where(row == STEPS * part + step_index, piece, tile)
                rest = rest - piece
        avg_out[...] = avg
        sq_out[...] = sq
        raw_keep[:rows, :] = jnp.where(first_role, raws[0], raws[1]).astype(jnp.bfloat16)
        raw_send[:rows, :] = jnp.where(first_role, raws[1], raws[0]).astype(jnp.bfloat16)
        raw_keep[rows:, :] = tile.astype(jnp.bfloat16)
        raw_send[rows:, :] = tile.astype(jnp.bfloat16)

    return pl.pallas_call(
        kernel,
        in_specs=[VMEM] * 4,
        out_specs=[VMEM] * 4,
        out_shape=[pltpu.VMEM(flat, jnp.float32)] * 2 + [pltpu.VMEM((rows + TILE, block_len), jnp.bfloat16)] * 2,
        compiler_params=SMALL,
        name="adam",
    )(*map(near_memory, (mine, got, exp_avg, exp_sq)))


def weights_update(weights, own, other, tiles, count_all, offsets, owners, columns, ready, orders, band_rows, width):
    row_blocks, col_blocks = offsets.shape
    block_len = columns.shape[-1] // 2
    size = own[0].shape[0]
    pieces = len(own)
    stride = size * pieces >> len(orders[0])
    shift = (size // stride).bit_length() - 1
    shards = tiles.shape[0] + 1
    owned = col_blocks >> len(orders[0])
    chunks = col_blocks // width
    span = width * block_len
    count = len(ready)

    def kernel(offsets_ref, owners_ref, tiles_ref, weights_ref, columns_ref, *refs):
        piece_refs = [refs[:pieces], refs[pieces:2 * pieces]]
        ready_refs = refs[2 * pieces:2 * pieces + count]
        refs = refs[2 * pieces + count:]
        out_hbm, scales_ref, ready_hbm = refs[0], refs[1], refs[2:2 + count]
        groups_ref, out_ref, departures, leaving, *scatters = refs[2 + count:]
        device = lax.axis_index("wide")
        role = device & 1
        first_role = role == 0
        copies = [
            pltpu.make_async_copy(source, target, leaving.at[index])
            for index, (source, target) in enumerate(zip(ready_refs, ready_hbm))
        ]
        for copy in copies:
            copy.start()
        fill_groups(groups_ref, orders)
        scatters = clear(scatters)
        scales = []
        rows = [[ref[begin + stride - TILE:begin + stride, :] for ref in piece_refs[0] for begin in range(0, size, stride)]]
        for shard in range(shards - 1):
            rows.append([tiles_ref[shard, group] for group in range(1 << len(orders[0]))])
        tile = tree_sum([axis_sum([value.astype(jnp.float32) for value in values], orders, first_role) for values in rows])
        parity = lax.broadcasted_iota(jnp.int32, tile.shape, 0) & 1
        for step_index in range(STEPS):
            power = jnp.sum(jnp.where(parity == step_index, tile, 0.0), keepdims=True)
            scales.append(jnp.broadcast_to(jnp.sqrt(power / count_all + rms_eps), (1, block_len)))
        inverses = [1.0 / scale for scale in scales]
        factors = [jnp.broadcast_to(factor, (band_rows, block_len)) for factor in (
            jnp.where(first_role, inverses[0], inverses[1]), jnp.where(first_role, inverses[1], inverses[0]))]

        def tile_of(part):
            row, chunk = block_of(part, chunks, row_blocks)
            return (pl.ds(pl.multiple_of(row * block_len, block_len), block_len),
                    pl.ds(pl.multiple_of(chunk * span, span), span))

        def departure(part):
            tile = tile_of(part)
            return pltpu.make_async_copy(out_ref.at[tile], out_hbm.at[tile], departures.at[part])

        def body(part, carry):
            row, chunk = block_of(part, chunks, row_blocks)
            totals = []
            for index in range(width):
                slot = owners_ref[row, chunk * width + index]
                owner, within = owner_of(slot, owned)
                within = (row * owned + within) * band_rows
                total = jnp.zeros((band_rows, block_len), jnp.float32)
                for number in range(STEPS):
                    group = groups_ref[role ^ number, owner ^ device ^ number]
                    which = group >> shift
                    rows = pl.ds(pl.multiple_of((group & ((1 << shift) - 1)) * stride + within, TILE), band_rows)
                    raw = piece_refs[number][0][rows, :]
                    for piece in range(1, pieces):
                        raw = jnp.where(which == piece, piece_refs[number][piece][rows, :], raw)
                    total = total + raw.astype(jnp.float32) * factors[number]
                totals.append(total)
            right = right_dot(jnp.concatenate(totals, 0), columns_ref[0])
            ranges = [pl.ds(offsets_ref[row, chunk * width + index], band_rows) for index in range(width)]
            values = [right[index * band_rows:(index + 1) * band_rows] for index in range(width)]
            inverse = left_dot(columns_ref, scatters, ranges, values)
            tile = tile_of(part)
            out_ref[tile] = (weights_ref[tile].astype(jnp.float32) - learning_rate * inverse).astype(out_ref.dtype)
            departure(part).start()
            return carry

        lax.fori_loop(0, row_blocks * chunks, body, 0)
        for step_index in range(STEPS):
            scales_ref[step_index] = scales[step_index][0, 0]
        for part in range(row_blocks * chunks):
            departure(part).wait()
        for copy in copies:
            copy.wait()

    return pl.pallas_call(
        kernel,
        in_specs=[SMEM, SMEM] + [VMEM] * (3 + 2 * pieces + count),
        out_specs=[HBM, SMEM] + [HBM] * count,
        out_shape=[
            pltpu.HBM(weights.shape, weights.dtype),
            jax.ShapeDtypeStruct((STEPS,), jnp.float32),
        ] + [pltpu.HBM(value.shape, value.dtype) for value in ready],
        scratch_shapes=[
            pltpu.SMEM((STEPS, 1 << len(orders[0])), jnp.int32),
            pltpu.VMEM(weights.shape, weights.dtype),
            pltpu.SemaphoreType.DMA((row_blocks * chunks,)),
            pltpu.SemaphoreType.DMA((count,)),
        ] + [pltpu.VMEM((block_len, block_len), jnp.float32)] * (2 * width),
        compiler_params=SMALL,
        name="weights_update",
    )(offsets, owners, *map(near_memory, (tiles, weights, columns, *own, *other, *ready)))


def swap(value, orders, stage):
    pairs = [(index, index ^ (1 << orders[index & 1][stage])) for index in range(1 << len(orders[0]))]
    return lax.ppermute(value, "wide", pairs)


def across(value, orders, stage, shift, shards):
    pairs = []
    for index in range(1 << len(orders[0])):
        partner = index if stage is None else index ^ (1 << orders[index & 1][stage])
        pairs += [(index * shards + shard, partner * shards + (shard ^ shift)) for shard in range(shards)]
    return lax.ppermute(value, ("wide", "shard"), pairs)


def axis_sum(values, orders, first_role):
    sums = []
    for order in orders:
        entries = {}
        for place, value in enumerate(values):
            digits = [place >> (len(order) - 1 - position) & 1 for position in range(len(order))]
            entries[sum(digit << bit for digit, bit in zip(digits, order))] = value
        current = [entries[index] for index in range(len(values))]
        sums.append(tree_sum(current))
    return jnp.where(first_role, *sums)


def tree_sum(values):
    while len(values) > 1:
        values = [a + b for a, b in zip(values[::2], values[1::2])]
    return values[0]


def per_device(weights, momentum, grads, offsets, owners, exp_avg, exp_sq):
    row_blocks, owned, band_rows, block_len = exp_avg.shape
    replicas = lax.axis_size("wide")
    shards = lax.axis_size("shard")
    count_all = exp_avg.size * replicas * shards
    table = dct_table(block_len)
    picks = jnp.asarray(row_tables(table))
    columns = jnp.asarray(column_tables(table))
    width = 16
    bits = replicas.bit_length() - 1
    orders = [list(range(1, bits)) + [0] for _ in range(STEPS)]
    if bits > 3:
        orders[1][:2] = orders[1][1::-1]
    core = bits - 1
    near_momentum, near_grads, taken, kept, sent = bands(
        momentum[0], grads[:, 0], offsets, owners, picks, columns, band_rows, orders, width)
    new_momentum = momentum_update(near_momentum, near_grads, taken, offsets, columns, band_rows, width)
    got = swap(sent, orders, core)
    kept = kept + got.astype(jnp.float32)
    middle = kept.shape[0] // 2
    keep, send = kept[:middle], kept[middle:]
    for stage in range(core):
        middle = send.shape[0] // 2
        if stage == core - 1:
            keep = keep + swap(send.astype(jnp.bfloat16), orders, stage).astype(jnp.float32)
            keep, send = keep[:middle], keep[middle:]
            break
        high = swap(send[middle:].astype(jnp.bfloat16), orders, stage)
        low = swap(send[:middle].astype(jnp.bfloat16), orders, stage)
        send = keep[middle:] + high.astype(jnp.float32)
        low, _ = lax.optimization_barrier((low, send))
        keep = keep[:middle] + low.astype(jnp.float32)
    got = swap(send, orders, core)
    flat = (row_blocks * owned, band_rows, block_len)
    avg_now, sq_now, raw, raw_other = adam(keep, got, exp_avg.reshape(flat), exp_sq.reshape(flat), replicas)
    far = swap(raw_other, orders, core)
    nears, fars = [], [jnp.concatenate([raw, far], 0)]
    for stage in reversed(range(core)):
        nears = [jnp.concatenate(values, 0) if len(values) > 1 else values[0] for values in (nears, fars) if values]
        fars = []
        for value in nears:
            fars.append(swap(value, orders, stage))
    tiles = jnp.concatenate([value.reshape(-1, raw.shape[0], block_len)[:, -TILE:] for value in nears], 0)
    tiles = jnp.stack([
        jnp.concatenate([across(tiles, orders, turn, shift, shards) for turn in (None, 0)], 0)
        for shift in range(1, shards)])
    own = nears + fars
    other = [swap(value, orders, core) for value in own]
    new_weights, scales, new_momentum, avg_now, sq_now = weights_update(
        weights, own, other, tiles, count_all, offsets, owners, columns, (new_momentum, avg_now, sq_now), orders, band_rows, width)
    return (new_weights, new_momentum[None], avg_now.reshape(exp_avg.shape), sq_now.reshape(exp_sq.shape), scales)


def solution(mesh):
    in_specs = (
        P("shard", None),
        P("wide", "shard", None),
        P(None, "wide", "shard", None),
        P("shard", None),
        P("shard", None),
        P("shard", "wide", None, None),
        P("shard", "wide", None, None),
    )
    out_specs = (
        P("shard", None),
        P("wide", "shard", None),
        P("shard", "wide", None, None),
        P("shard", "wide", None, None),
        P(),
    )
    return jax.shard_map(per_device, mesh=mesh, in_specs=in_specs, out_specs=out_specs, check_vma=False)
```

```python
import jax
import jax.numpy as jnp
import numpy as np
from jax import lax
from jax.experimental import pallas as pl
from jax.experimental.pallas import tpu as pltpu
from jax.sharding import PartitionSpec as P


STEPS = 2
TILE = 16

momentum_decay = 0.9
beta_one = 0.8
beta_two = 0.95
adam_eps = 1e-08
rms_eps = 1e-06
learning_rate = 0.2


SMEM = pl.BlockSpec(memory_space=pltpu.SMEM)
VMEM = pl.BlockSpec(memory_space=pltpu.VMEM)
ANY = pl.BlockSpec(memory_space=pl.ANY)
HBM = pl.BlockSpec(memory_space=pltpu.HBM)
SMALL = pltpu.CompilerParams(vmem_limit_bytes=20 << 20)


def dct_table(length):
    frequency = np.arange(length, dtype=np.float64)[:, None]
    position = np.arange(length, dtype=np.float64)[None, :]
    cosines = np.cos(np.pi * (2.0 * position + 1.0) * frequency / (2.0 * length))
    scaling = np.where(frequency == 0.0, np.sqrt(1.0 / length), np.sqrt(2.0 / length))
    return (cosines * scaling).astype(np.float32)


def split_table(table):
    high = table.astype(jnp.bfloat16)
    low = (table - high.astype(np.float32)).astype(jnp.bfloat16)
    return high, low


def row_tables(table):
    high, low = split_table(table)
    decayed_high, decayed_low = split_table(np.float32(momentum_decay) * table)
    wide = table.astype(np.float64)
    residue = momentum_decay * (np.eye(len(table)) - wide @ wide.T)
    parts = (high, low, decayed_high, decayed_low, residue.astype(np.float32).astype(jnp.bfloat16))
    return np.stack([part.astype(np.float32) for part in parts])


def column_tables(table):
    high, low = split_table(table)
    zero = np.zeros_like(low)
    rights = [np.block([[h, l], [h, zero]]) for h, l in ((high, low), (high.T, low.T))]
    lefts = np.block([[high.T, high.T], [low.T, zero]])
    return np.stack([*rights, lefts])


def near_memory(value):
    return pltpu.with_memory_space_constraint(value, pltpu.VMEM)


def far_memory(value):
    return pltpu.with_memory_space_constraint(value, pltpu.HBM)


def halves(value):
    high = value.astype(jnp.bfloat16)
    return high, (value - high.astype(jnp.float32)).astype(jnp.bfloat16)


def dot(left, right):
    return jnp.dot(left, right, preferred_element_type=jnp.float32)


def right_dot(left, table):
    length = left.shape[1]
    both = dot(jnp.concatenate(halves(left), 1), table)
    return both[:, :length] + both[:, length:]


def block_of(part, chunks, row_blocks):
    return (0, part) if row_blocks == 1 else (part // chunks, part % chunks)


def fill_groups(groups_ref, orders):
    for role, order in enumerate(orders):
        for relative in range(1 << len(order)):
            place = 0
            for bit in order:
                place = place * 2 + ((relative >> bit) & 1)
            groups_ref[role, relative] = place


def owner_of(slot, owned):
    if owned & (owned - 1) == 0:
        return slot >> (owned.bit_length() - 1), slot & (owned - 1)
    return lax.div(slot, owned), lax.rem(slot, owned)


def slot_places(groups_ref, slot, device, row, owned, size):
    owner, within = owner_of(slot, owned)
    relative = owner ^ device
    role = device & 1
    within = row * owned + within
    return groups_ref[role, relative] * size + within, groups_ref[1 - role, relative ^ 1] * size + within


def bands(momentum, grads, offsets, owners, picks, columns, band_rows, orders, width):
    row_blocks, col_blocks = offsets.shape
    block_len = picks.shape[-1]
    owned = col_blocks >> len(orders[0])
    slots = row_blocks * col_blocks
    chunks = col_blocks // width
    span = width * block_len

    def kernel(offsets_hbm, owners_hbm, momentum_hbm, grads_hbm, picks_hbm, columns_hbm, momentum_ref, grads_ref, taken_ref,
               keep_ref, send_ref, offsets_ref, owners_ref, groups_ref, picks_ref, columns_ref, lefts, tables, arrivals, *scatters):
        device = lax.axis_index("wide")
        first_role = (device & 1) == 0
        small = [
            pltpu.make_async_copy(source, target, tables.at[index])
            for index, (source, target) in enumerate([
                (offsets_hbm, offsets_ref), (owners_hbm, owners_ref), (picks_hbm, picks_ref), (columns_hbm, columns_ref)])
        ]
        for copy in small:
            copy.start()

        def arrival(part):
            row, chunk = block_of(part, chunks, row_blocks)
            rows = pl.ds(row * block_len, block_len)
            lanes = pl.ds(chunk * span, span)
            return [
                pltpu.make_async_copy(momentum_hbm.at[rows, lanes], momentum_ref.at[rows, lanes], arrivals.at[0, part]),
                pltpu.make_async_copy(grads_hbm.at[:, rows, lanes], grads_ref.at[:, rows, lanes], arrivals.at[1, part]),
            ]

        for part in range(row_blocks * chunks):
            for copy in arrival(part):
                copy.start()
        fill_groups(groups_ref, orders)
        blank = jnp.zeros((band_rows, block_len), jnp.float32)
        for scatter in scatters:
            scatter[...] = jnp.zeros_like(scatter)
        for copy in small:
            copy.wait()

        def body(part, carry):
            for copy in arrival(part):
                copy.wait()
            row, chunk = block_of(part, chunks, row_blocks)
            block_rows = slice(0, block_len) if row_blocks == 1 else pl.ds(pl.multiple_of(row * block_len, block_len), block_len)
            taken_start = part * width * band_rows
            ranges = [pl.ds(offsets_ref[row, chunk * width + index], band_rows) for index in range(width)]
            columns_of = [
                pl.ds(pl.multiple_of((chunk * width + index) * block_len, block_len), block_len) for index in range(width)]
            for index, (rows, lanes) in enumerate(zip(ranges, columns_of)):
                high, low, decayed_high, decayed_low = [picks_ref[number, rows, :].astype(jnp.bfloat16) for number in range(4)]
                first = jnp.concatenate(
                    [jnp.concatenate([decayed_high, high], 1), jnp.concatenate([decayed_low, low], 1)], 0)
                pair = dot(first, jnp.concatenate([momentum_ref[block_rows, lanes], grads_ref[0, block_rows, lanes]], 0))
                left = pair[:band_rows] + pair[band_rows:]
                scatters[index][rows, :] = left
                lefts[index * band_rows:(index + 1) * band_rows, :] = left
            for index, (rows, lanes) in enumerate(zip(ranges, columns_of)):
                high, low, residue = [picks_ref[number, rows, :].astype(jnp.bfloat16) for number in (0, 1, 4)]
                second = jnp.concatenate(
                    [jnp.concatenate([high, residue], 1), jnp.concatenate([low, jnp.zeros_like(low)], 1)], 0)
                pair = dot(second, jnp.concatenate(
                    [grads_ref[1, block_rows, lanes], scatters[index][...].astype(jnp.bfloat16)], 0))
                scatters[index][rows, :] = blank
                left = pair[:band_rows] + pair[band_rows:]
                lefts[(width + index) * band_rows:(width + index + 1) * band_rows, :] = left
                taken_ref[pl.ds(pl.multiple_of(taken_start + index * band_rows, band_rows), band_rows), :] = (
                    momentum_decay * lefts[index * band_rows:(index + 1) * band_rows, :] + left)
            band = right_dot(lefts[...], columns_ref[1])
            for index in range(width):
                slot = owners_ref[row, chunk * width + index]
                here, there = slot_places(groups_ref, slot, device, row, owned, row_blocks * owned)
                values = [band[(step_index * width + index) * band_rows:(step_index * width + index + 1) * band_rows]
                          for step_index in range(STEPS)]
                keep_ref[here] = jnp.where(first_role, values[0], values[1])
                send_ref[there] = jnp.where(first_role, values[1], values[0]).astype(jnp.bfloat16)
            return carry

        lax.fori_loop(0, row_blocks * chunks, body, 0)

    shape = (slots, band_rows, block_len)
    return pl.pallas_call(
        kernel,
        in_specs=[HBM] * 6,
        out_specs=[VMEM] * 5,
        out_shape=[
            pltpu.VMEM(momentum.shape, momentum.dtype),
            pltpu.VMEM(grads.shape, grads.dtype),
            pltpu.VMEM((slots * band_rows, block_len), jnp.float32),
            pltpu.VMEM(shape, jnp.float32),
            pltpu.VMEM(shape, jnp.bfloat16),
        ],
        scratch_shapes=[
            pltpu.SMEM(offsets.shape, offsets.dtype),
            pltpu.SMEM(owners.shape, owners.dtype),
            pltpu.SMEM((STEPS, 1 << len(orders[0])), jnp.int32),
            pltpu.VMEM(picks.shape, picks.dtype),
            pltpu.VMEM(columns.shape, columns.dtype),
            pltpu.VMEM((STEPS * width * band_rows, block_len), jnp.float32),
            pltpu.SemaphoreType.DMA((4,)),
            pltpu.SemaphoreType.DMA((2, row_blocks * chunks)),
        ] + [pltpu.VMEM((block_len, block_len), jnp.float32)] * width,
        compiler_params=SMALL,
        name="bands",
    )(*map(far_memory, (offsets, owners, momentum, grads, picks, columns)))


def left_dot(columns_ref, scatters, ranges, values):
    blank = jnp.zeros_like(values[0])
    highs = []
    lows = []
    for (high_ref, low_ref), rows, value in zip(scatters, ranges, values):
        high = value.astype(jnp.bfloat16).astype(jnp.float32)
        high_ref[rows, :] = high
        low_ref[rows, :] = value - high
        highs.append(high_ref[...].astype(jnp.bfloat16))
        lows.append(low_ref[...].astype(jnp.bfloat16))
        high_ref[rows, :] = blank
        low_ref[rows, :] = blank
    high = jnp.concatenate(highs, 1)
    low = jnp.concatenate(lows, 1)
    length = high.shape[0]
    return dot(columns_ref[2, :length], jnp.concatenate([high, low], 0)) + dot(columns_ref[2, length:, :length], high)


def clear(scatters):
    for part in scatters:
        part[...] = jnp.zeros_like(part)
    return list(zip(scatters[::2], scatters[1::2]))


def momentum_update(momentum, grads, taken, offsets, columns, band_rows, width):
    row_blocks, col_blocks = offsets.shape
    block_len = columns.shape[-1] // 2
    chunks = col_blocks // width
    span = width * block_len

    def kernel(offsets_ref, momentum_ref, grads_ref, taken_ref, columns_ref, out_ref, *scatters):
        scatters = clear(scatters)

        def body(part, carry):
            row, chunk = block_of(part, chunks, row_blocks)
            ranges = [pl.ds(offsets_ref[row, chunk * width + index], band_rows) for index in range(width)]
            values = [
                taken_ref[pl.ds(pl.multiple_of((part * width + index) * band_rows, band_rows), band_rows), :]
                for index in range(width)]
            inverse = left_dot(columns_ref, scatters, ranges, values)
            tile = (pl.ds(pl.multiple_of(row * block_len, block_len), block_len),
                    pl.ds(pl.multiple_of(chunk * span, span), span))
            blended = momentum_decay * momentum_ref[tile].astype(jnp.float32) + grads_ref[(0,) + tile].astype(jnp.float32)
            blended = momentum_decay * blended + grads_ref[(1,) + tile].astype(jnp.float32)
            out_ref[tile] = (blended - inverse).astype(out_ref.dtype)
            return carry

        lax.fori_loop(0, row_blocks * chunks, body, 0)

    return pl.pallas_call(
        kernel,
        in_specs=[SMEM] + [VMEM] * 4,
        out_specs=VMEM,
        out_shape=pltpu.VMEM(momentum.shape, momentum.dtype),
        scratch_shapes=[pltpu.VMEM((block_len, block_len), jnp.float32)] * (2 * width),
        compiler_params=SMALL,
        name="momentum_update",
    )(offsets, *map(near_memory, (momentum, grads, taken, columns)))


def adam(mine, got, exp_avg, exp_sq, others, replicas):
    flat = exp_avg.shape
    count = flat[0]
    block_len = flat[-1]
    rows = flat[0] * flat[1]

    def kernel(mine_ref, got_ref, avg_ref, sq_ref, others_ref, avg_out, sq_out, raw_out):
        first_role = (lax.axis_index("wide") & 1) == 0
        row = lax.broadcasted_iota(jnp.int32, (TILE, block_len), 0)
        powers = []
        for core, (avg, sq) in enumerate(((avg_ref[...], sq_ref[...]), (others_ref[0], others_ref[1]))):
            own = mine_ref[core * count:(core + 1) * count]
            other = got_ref[(1 - core) * count:(2 - core) * count]
            raws = []
            for total in (jnp.where(first_role, own, other), jnp.where(first_role, other, own)):
                mean_band = total / replicas
                avg = beta_one * avg + (1.0 - beta_one) * mean_band
                sq = beta_two * sq + (1.0 - beta_two) * mean_band * mean_band
                raws.append((avg / (jnp.sqrt(sq) + adam_eps)).reshape(rows, block_len))
            if core == 0:
                avg_out[...] = avg
                sq_out[...] = sq
            raw_out[core * rows:(core + 1) * rows, :] = jnp.where(first_role, raws[0], raws[1]).astype(jnp.bfloat16)
            powers.append([jnp.sum(raw * raw, axis=0, keepdims=True) for raw in raws])
        tile = jnp.zeros((TILE, block_len), jnp.float32)
        for step_index in range(STEPS):
            rest = powers[0][step_index] + powers[1][step_index]
            for part in range(3):
                piece = rest.astype(jnp.bfloat16).astype(jnp.float32)
                tile = jnp.where(row == STEPS * part + step_index, piece, tile)
                rest = rest - piece
        raw_out[2 * rows:, :] = tile.astype(jnp.bfloat16)

    return pl.pallas_call(
        kernel,
        in_specs=[VMEM] * 5,
        out_specs=[VMEM] * 3,
        out_shape=[pltpu.VMEM(flat, jnp.float32)] * 2 + [pltpu.VMEM((2 * rows + TILE, block_len), jnp.bfloat16)],
        compiler_params=SMALL,
        name="adam",
    )(*map(near_memory, (mine, got, exp_avg, exp_sq, others)))


def weights_update(weights, own, other, tiles, count_all, offsets, owners, columns, ready, orders, band_rows, width):
    row_blocks, col_blocks = offsets.shape
    block_len = columns.shape[-1] // 2
    size = own[0].shape[0]
    pieces = len(own)
    stride = 2 * size * pieces >> len(orders[0])
    shift = (size // stride).bit_length() - 1
    shards = tiles.shape[0] + 1
    owned = col_blocks >> len(orders[0])
    chunks = col_blocks // width
    span = width * block_len
    count = len(ready)

    def kernel(offsets_ref, owners_ref, tiles_ref, weights_ref, columns_ref, *refs):
        piece_refs = [refs[:pieces], refs[pieces:2 * pieces]]
        ready_refs = refs[2 * pieces:2 * pieces + count]
        refs = refs[2 * pieces + count:]
        out_hbm, scales_ref, ready_hbm = refs[0], refs[1], refs[2:2 + count]
        groups_ref, out_ref, departures, leaving, *scatters = refs[2 + count:]
        device = lax.axis_index("wide")
        role = device & 1
        first_role = role == 0
        copies = [
            pltpu.make_async_copy(source, target, leaving.at[index])
            for index, (source, target) in enumerate(zip(ready_refs, ready_hbm))
        ]
        for copy in copies:
            copy.start()
        fill_groups(groups_ref, orders)
        scatters = clear(scatters)
        scales = []
        rows = [[ref[begin + stride - TILE:begin + stride, :] for ref in piece_refs[0] for begin in range(0, size, stride)]]
        for shard in range(shards - 1):
            rows.append([tiles_ref[shard, group] for group in range(1 << len(orders[0]) - 1)])
        tile = tree_sum([axis_sum([value.astype(jnp.float32) for value in values], [order[:-1] for order in orders], first_role) for values in rows])
        parity = lax.broadcasted_iota(jnp.int32, tile.shape, 0) & 1
        for step_index in range(STEPS):
            power = jnp.sum(jnp.where(parity == step_index, tile, 0.0), keepdims=True)
            scales.append(jnp.broadcast_to(jnp.sqrt(power / count_all + rms_eps), (1, block_len)))
        inverses = [1.0 / scale for scale in scales]
        factors = [jnp.broadcast_to(factor, (band_rows, block_len)) for factor in (
            jnp.where(first_role, inverses[0], inverses[1]), jnp.where(first_role, inverses[1], inverses[0]))]

        def tile_of(part):
            row, chunk = block_of(part, chunks, row_blocks)
            return (pl.ds(pl.multiple_of(row * block_len, block_len), block_len),
                    pl.ds(pl.multiple_of(chunk * span, span), span))

        def departure(part):
            tile = tile_of(part)
            return pltpu.make_async_copy(out_ref.at[tile], out_hbm.at[tile], departures.at[part])

        def body(part, carry):
            row, chunk = block_of(part, chunks, row_blocks)
            totals = []
            for index in range(width):
                slot = owners_ref[row, chunk * width + index]
                owner, within = owner_of(slot, owned)
                within = (row * owned + within) * band_rows
                total = jnp.zeros((band_rows, block_len), jnp.float32)
                for number in range(STEPS):
                    group = groups_ref[role ^ number, owner ^ device ^ number]
                    chip = group >> 1
                    which = chip >> shift
                    begin = (chip & ((1 << shift) - 1)) * stride + (group & 1) * (row_blocks * owned * band_rows) + within
                    rows = pl.ds(pl.multiple_of(begin, TILE), band_rows)
                    raw = piece_refs[number][0][rows, :]
                    for piece in range(1, pieces):
                        raw = jnp.where(which == piece, piece_refs[number][piece][rows, :], raw)
                    total = total + raw.astype(jnp.float32) * factors[number]
                totals.append(total)
            right = right_dot(jnp.concatenate(totals, 0), columns_ref[0])
            ranges = [pl.ds(offsets_ref[row, chunk * width + index], band_rows) for index in range(width)]
            values = [right[index * band_rows:(index + 1) * band_rows] for index in range(width)]
            inverse = left_dot(columns_ref, scatters, ranges, values)
            tile = tile_of(part)
            out_ref[tile] = (weights_ref[tile].astype(jnp.float32) - learning_rate * inverse).astype(out_ref.dtype)
            departure(part).start()
            return carry

        lax.fori_loop(0, row_blocks * chunks, body, 0)
        for step_index in range(STEPS):
            scales_ref[step_index] = scales[step_index][0, 0]
        for part in range(row_blocks * chunks):
            departure(part).wait()
        for copy in copies:
            copy.wait()

    return pl.pallas_call(
        kernel,
        in_specs=[SMEM, SMEM] + [VMEM] * (3 + 2 * pieces + count),
        out_specs=[HBM, SMEM] + [HBM] * count,
        out_shape=[
            pltpu.HBM(weights.shape, weights.dtype),
            jax.ShapeDtypeStruct((STEPS,), jnp.float32),
        ] + [pltpu.HBM(value.shape, value.dtype) for value in ready],
        scratch_shapes=[
            pltpu.SMEM((STEPS, 1 << len(orders[0])), jnp.int32),
            pltpu.VMEM(weights.shape, weights.dtype),
            pltpu.SemaphoreType.DMA((row_blocks * chunks,)),
            pltpu.SemaphoreType.DMA((count,)),
        ] + [pltpu.VMEM((block_len, block_len), jnp.float32)] * (2 * width),
        compiler_params=SMALL,
        name="weights_update",
    )(offsets, owners, *map(near_memory, (tiles, weights, columns, *own, *other, *ready)))


def swap(value, orders, stage):
    pairs = [(index, index ^ (1 << orders[index & 1][stage])) for index in range(1 << len(orders[0]))]
    return lax.ppermute(value, "wide", pairs)


def across(value, orders, stage, shift, shards):
    pairs = []
    for index in range(1 << len(orders[0])):
        partner = index if stage is None else index ^ (1 << orders[index & 1][stage])
        pairs += [(index * shards + shard, partner * shards + (shard ^ shift)) for shard in range(shards)]
    return lax.ppermute(value, ("wide", "shard"), pairs)


def axis_sum(values, orders, first_role):
    sums = []
    for order in orders:
        entries = {}
        for place, value in enumerate(values):
            digits = [place >> (len(order) - 1 - position) & 1 for position in range(len(order))]
            entries[sum(digit << bit - 1 for digit, bit in zip(digits, order))] = value
        current = [entries[index] for index in range(len(values))]
        sums.append(tree_sum(current))
    return jnp.where(first_role, *sums)


def tree_sum(values):
    while len(values) > 1:
        values = [a + b for a, b in zip(values[::2], values[1::2])]
    return values[0]


def per_device(weights, momentum, grads, offsets, owners, exp_avg, exp_sq):
    row_blocks, owned, band_rows, block_len = exp_avg.shape
    replicas = lax.axis_size("wide")
    shards = lax.axis_size("shard")
    count_all = exp_avg.size * replicas * shards
    table = dct_table(block_len)
    picks = jnp.asarray(row_tables(table))
    columns = jnp.asarray(column_tables(table))
    width = 16
    bits = replicas.bit_length() - 1
    orders = [list(range(1, bits)) + [0] for _ in range(STEPS)]
    if bits > 3:
        orders[1][:2] = orders[1][1::-1]
    core = bits - 1
    near_momentum, near_grads, taken, kept, sent = bands(
        momentum[0], grads[:, 0], offsets, owners, picks, columns, band_rows, orders, 2 * width)
    new_momentum = momentum_update(near_momentum, near_grads, taken, offsets, columns, band_rows, width)
    middle = kept.shape[0] // 2
    high = swap(sent[middle:], orders, core)
    low = swap(sent[:middle], orders, core)
    send = kept[middle:] + high.astype(jnp.float32)
    low, _ = lax.optimization_barrier((low, send))
    keep = kept[:middle] + low.astype(jnp.float32)
    for stage in range(core):
        middle = send.shape[0] // 2
        if stage == core - 1:
            keep = keep + swap(send.astype(jnp.bfloat16), orders, stage).astype(jnp.float32)
            break
        high = swap(send[middle:].astype(jnp.bfloat16), orders, stage)
        low = swap(send[:middle].astype(jnp.bfloat16), orders, stage)
        send = keep[middle:] + high.astype(jnp.float32)
        low, _ = lax.optimization_barrier((low, send))
        keep = keep[:middle] + low.astype(jnp.float32)
    flat = (row_blocks * owned, band_rows, block_len)
    exp_avg_now, exp_sq_now = exp_avg.reshape(flat), exp_sq.reshape(flat)
    others = swap(jnp.stack([exp_avg_now, exp_sq_now]), orders, core)
    got = swap(keep, orders, core)
    avg_now, sq_now, raw = adam(keep, got, exp_avg_now, exp_sq_now, others, replicas)
    nears, fars = [], [raw]
    for stage in reversed(range(core)):
        nears = [jnp.concatenate(values, 0) if len(values) > 1 else values[0] for values in (nears, fars) if values]
        fars = []
        for value in nears:
            fars.append(swap(value, orders, stage))
    tiles = jnp.concatenate([value.reshape(-1, raw.shape[0], block_len)[:, -TILE:] for value in nears], 0)
    tiles = jnp.stack([
        jnp.concatenate([across(tiles, orders, turn, shift, shards) for turn in (None, 0)], 0)
        for shift in range(1, shards)])
    own = nears + fars
    other = [swap(value, orders, core) for value in own]
    new_weights, scales, new_momentum, avg_now, sq_now = weights_update(
        weights, own, other, tiles, count_all, offsets, owners, columns, (new_momentum, avg_now, sq_now), orders, band_rows, width)
    return (new_weights, new_momentum[None], avg_now.reshape(exp_avg.shape), sq_now.reshape(exp_sq.shape), scales)


def solution(mesh):
    in_specs = (
        P("shard", None),
        P("wide", "shard", None),
        P(None, "wide", "shard", None),
        P("shard", None),
        P("shard", None),
        P("shard", "wide", None, None),
        P("shard", "wide", None, None),
    )
    out_specs = (
        P("shard", None),
        P("wide", "shard", None),
        P("shard", "wide", None, None),
        P("shard", "wide", None, None),
        P(),
    )
    return jax.shard_map(per_device, mesh=mesh, in_specs=in_specs, out_specs=out_specs, check_vma=False)
```

```python
import jax
import jax.numpy as jnp
import numpy as np
from jax import lax
from jax.experimental import pallas as pl
from jax.experimental.pallas import tpu as pltpu
from jax.sharding import PartitionSpec as P


STEPS = 2
TILE = 16

momentum_decay = 0.9
beta_one = 0.8
beta_two = 0.95
adam_eps = 1e-08
rms_eps = 1e-06
learning_rate = 0.2


SMEM = pl.BlockSpec(memory_space=pltpu.SMEM)
VMEM = pl.BlockSpec(memory_space=pltpu.VMEM)
ANY = pl.BlockSpec(memory_space=pl.ANY)
HBM = pl.BlockSpec(memory_space=pltpu.HBM)
SMALL = pltpu.CompilerParams(vmem_limit_bytes=20 << 20)


def dct_table(length):
    frequency = np.arange(length, dtype=np.float64)[:, None]
    position = np.arange(length, dtype=np.float64)[None, :]
    cosines = np.cos(np.pi * (2.0 * position + 1.0) * frequency / (2.0 * length))
    scaling = np.where(frequency == 0.0, np.sqrt(1.0 / length), np.sqrt(2.0 / length))
    return (cosines * scaling).astype(np.float32)


def split_table(table):
    high = table.astype(jnp.bfloat16)
    low = (table - high.astype(np.float32)).astype(jnp.bfloat16)
    return high, low


def row_tables(table):
    high, low = split_table(table)
    decayed_high, decayed_low = split_table(np.float32(momentum_decay) * table)
    wide = table.astype(np.float64)
    residue = momentum_decay * (np.eye(len(table)) - wide @ wide.T)
    parts = (high, low, decayed_high, decayed_low, residue.astype(np.float32).astype(jnp.bfloat16))
    return np.stack([part.astype(np.float32) for part in parts])


def column_tables(table):
    high, low = split_table(table)
    zero = np.zeros_like(low)
    rights = [np.block([[h, l], [h, zero]]) for h, l in ((high, low), (high.T, low.T))]
    lefts = np.block([[high.T, high.T], [low.T, zero]])
    return np.stack([*rights, lefts])


def near_memory(value):
    return pltpu.with_memory_space_constraint(value, pltpu.VMEM)


def far_memory(value):
    return pltpu.with_memory_space_constraint(value, pltpu.HBM)


def halves(value):
    high = value.astype(jnp.bfloat16)
    return high, (value - high.astype(jnp.float32)).astype(jnp.bfloat16)


def dot(left, right):
    return jnp.dot(left, right, preferred_element_type=jnp.float32)


def right_dot(left, table):
    length = left.shape[1]
    both = dot(jnp.concatenate(halves(left), 1), table)
    return both[:, :length] + both[:, length:]


def block_of(part, chunks, row_blocks):
    return (0, part) if row_blocks == 1 else (part // chunks, part % chunks)


def fill_groups(groups_ref, orders):
    for role, order in enumerate(orders):
        for relative in range(1 << len(order)):
            place = 0
            for bit in order:
                place = place * 2 + ((relative >> bit) & 1)
            groups_ref[role, relative] = place


def owner_of(slot, owned):
    if owned & (owned - 1) == 0:
        return slot >> (owned.bit_length() - 1), slot & (owned - 1)
    return lax.div(slot, owned), lax.rem(slot, owned)


def slot_places(groups_ref, slot, device, row, owned, size):
    owner, within = owner_of(slot, owned)
    relative = owner ^ device
    role = device & 1
    within = row * owned + within
    return groups_ref[role, relative] * size + within, groups_ref[1 - role, relative ^ 1] * size + within


def bands(momentum, grads, offsets, owners, picks, columns, band_rows, orders, width):
    row_blocks, col_blocks = offsets.shape
    block_len = picks.shape[-1]
    owned = col_blocks >> len(orders[0])
    slots = row_blocks * col_blocks
    chunks = col_blocks // width
    span = width * block_len

    def kernel(offsets_hbm, owners_hbm, momentum_hbm, grads_hbm, picks_hbm, columns_hbm, momentum_ref, grads_ref, taken_ref,
               keep_ref, send_ref, offsets_ref, owners_ref, groups_ref, picks_ref, columns_ref, lefts, tables, arrivals, *scatters):
        device = lax.axis_index("wide")
        first_role = (device & 1) == 0
        small = [
            pltpu.make_async_copy(source, target, tables.at[index])
            for index, (source, target) in enumerate([
                (offsets_hbm, offsets_ref), (owners_hbm, owners_ref), (picks_hbm, picks_ref), (columns_hbm, columns_ref)])
        ]
        for copy in small:
            copy.start()

        def arrival(part):
            row, chunk = block_of(part, chunks, row_blocks)
            rows = pl.ds(row * block_len, block_len)
            lanes = pl.ds(chunk * span, span)
            return [
                pltpu.make_async_copy(momentum_hbm.at[rows, lanes], momentum_ref.at[rows, lanes], arrivals.at[0, part]),
                pltpu.make_async_copy(grads_hbm.at[:, rows, lanes], grads_ref.at[:, rows, lanes], arrivals.at[1, part]),
            ]

        for part in range(row_blocks * chunks):
            for copy in arrival(part):
                copy.start()
        fill_groups(groups_ref, orders)
        blank = jnp.zeros((band_rows, block_len), jnp.float32)
        for scatter in scatters:
            scatter[...] = jnp.zeros_like(scatter)
        for copy in small:
            copy.wait()

        def body(part, carry):
            for copy in arrival(part):
                copy.wait()
            row, chunk = block_of(part, chunks, row_blocks)
            block_rows = slice(0, block_len) if row_blocks == 1 else pl.ds(pl.multiple_of(row * block_len, block_len), block_len)
            taken_start = part * width * band_rows
            ranges = [pl.ds(offsets_ref[row, chunk * width + index], band_rows) for index in range(width)]
            columns_of = [
                pl.ds(pl.multiple_of((chunk * width + index) * block_len, block_len), block_len) for index in range(width)]
            for index, (rows, lanes) in enumerate(zip(ranges, columns_of)):
                high, low, decayed_high, decayed_low = [picks_ref[number, rows, :].astype(jnp.bfloat16) for number in range(4)]
                first = jnp.concatenate(
                    [jnp.concatenate([decayed_high, high], 1), jnp.concatenate([decayed_low, low], 1)], 0)
                pair = dot(first, jnp.concatenate([momentum_ref[block_rows, lanes], grads_ref[0, block_rows, lanes]], 0))
                left = pair[:band_rows] + pair[band_rows:]
                scatters[index][rows, :] = left
                lefts[index * band_rows:(index + 1) * band_rows, :] = left
            for index, (rows, lanes) in enumerate(zip(ranges, columns_of)):
                high, low, residue = [picks_ref[number, rows, :].astype(jnp.bfloat16) for number in (0, 1, 4)]
                second = jnp.concatenate(
                    [jnp.concatenate([high, residue], 1), jnp.concatenate([low, jnp.zeros_like(low)], 1)], 0)
                pair = dot(second, jnp.concatenate(
                    [grads_ref[1, block_rows, lanes], scatters[index][...].astype(jnp.bfloat16)], 0))
                scatters[index][rows, :] = blank
                left = pair[:band_rows] + pair[band_rows:]
                lefts[(width + index) * band_rows:(width + index + 1) * band_rows, :] = left
                taken_ref[pl.ds(pl.multiple_of(taken_start + index * band_rows, band_rows), band_rows), :] = (
                    momentum_decay * lefts[index * band_rows:(index + 1) * band_rows, :] + left)
            band = right_dot(lefts[...], columns_ref[1])
            for index in range(width):
                slot = owners_ref[row, chunk * width + index]
                here, there = slot_places(groups_ref, slot, device, row, owned, row_blocks * owned)
                values = [band[(step_index * width + index) * band_rows:(step_index * width + index + 1) * band_rows]
                          for step_index in range(STEPS)]
                keep_ref[here] = jnp.where(first_role, values[0], values[1])
                send_ref[there] = jnp.where(first_role, values[1], values[0]).astype(jnp.bfloat16)
            return carry

        lax.fori_loop(0, row_blocks * chunks, body, 0)

    shape = (slots, band_rows, block_len)
    return pl.pallas_call(
        kernel,
        in_specs=[HBM] * 6,
        out_specs=[VMEM] * 5,
        out_shape=[
            pltpu.VMEM(momentum.shape, momentum.dtype),
            pltpu.VMEM(grads.shape, grads.dtype),
            pltpu.VMEM((slots * band_rows, block_len), jnp.float32),
            pltpu.VMEM(shape, jnp.float32),
            pltpu.VMEM(shape, jnp.bfloat16),
        ],
        scratch_shapes=[
            pltpu.SMEM(offsets.shape, offsets.dtype),
            pltpu.SMEM(owners.shape, owners.dtype),
            pltpu.SMEM((STEPS, 1 << len(orders[0])), jnp.int32),
            pltpu.VMEM(picks.shape, picks.dtype),
            pltpu.VMEM(columns.shape, columns.dtype),
            pltpu.VMEM((STEPS * width * band_rows, block_len), jnp.float32),
            pltpu.SemaphoreType.DMA((4,)),
            pltpu.SemaphoreType.DMA((2, row_blocks * chunks)),
        ] + [pltpu.VMEM((block_len, block_len), jnp.float32)] * width,
        compiler_params=SMALL,
        name="bands",
    )(*map(far_memory, (offsets, owners, momentum, grads, picks, columns)))


def left_dot(columns_ref, scatters, ranges, values):
    blank = jnp.zeros_like(values[0])
    highs = []
    lows = []
    for (high_ref, low_ref), rows, value in zip(scatters, ranges, values):
        high = value.astype(jnp.bfloat16).astype(jnp.float32)
        high_ref[rows, :] = high
        low_ref[rows, :] = value - high
        highs.append(high_ref[...].astype(jnp.bfloat16))
        lows.append(low_ref[...].astype(jnp.bfloat16))
        high_ref[rows, :] = blank
        low_ref[rows, :] = blank
    high = jnp.concatenate(highs, 1)
    low = jnp.concatenate(lows, 1)
    length = high.shape[0]
    return dot(columns_ref[2, :length], jnp.concatenate([high, low], 0)) + dot(columns_ref[2, length:, :length], high)


def clear(scatters):
    for part in scatters:
        part[...] = jnp.zeros_like(part)
    return list(zip(scatters[::2], scatters[1::2]))


def momentum_update(momentum, grads, taken, offsets, columns, band_rows, width):
    row_blocks, col_blocks = offsets.shape
    block_len = columns.shape[-1] // 2
    chunks = col_blocks // width
    span = width * block_len

    def kernel(offsets_ref, momentum_ref, grads_ref, taken_ref, columns_ref, out_ref, *scatters):
        scatters = clear(scatters)

        def body(part, carry):
            row, chunk = block_of(part, chunks, row_blocks)
            ranges = [pl.ds(offsets_ref[row, chunk * width + index], band_rows) for index in range(width)]
            values = [
                taken_ref[pl.ds(pl.multiple_of((part * width + index) * band_rows, band_rows), band_rows), :]
                for index in range(width)]
            inverse = left_dot(columns_ref, scatters, ranges, values)
            tile = (pl.ds(pl.multiple_of(row * block_len, block_len), block_len),
                    pl.ds(pl.multiple_of(chunk * span, span), span))
            blended = momentum_decay * momentum_ref[tile].astype(jnp.float32) + grads_ref[(0,) + tile].astype(jnp.float32)
            blended = momentum_decay * blended + grads_ref[(1,) + tile].astype(jnp.float32)
            out_ref[tile] = (blended - inverse).astype(out_ref.dtype)
            return carry

        lax.fori_loop(0, row_blocks * chunks, body, 0)

    return pl.pallas_call(
        kernel,
        in_specs=[SMEM] + [VMEM] * 4,
        out_specs=VMEM,
        out_shape=pltpu.VMEM(momentum.shape, momentum.dtype),
        scratch_shapes=[pltpu.VMEM((block_len, block_len), jnp.float32)] * (2 * width),
        compiler_params=SMALL,
        name="momentum_update",
    )(offsets, *map(near_memory, (momentum, grads, taken, columns)))


def adam(mine, got, exp_avg, exp_sq, others, replicas):
    flat = exp_avg.shape
    count = flat[0]
    block_len = flat[-1]
    rows = flat[0] * flat[1]

    def kernel(mine_ref, got_ref, avg_ref, sq_ref, others_ref, avg_out, sq_out, raw_out):
        first_role = (lax.axis_index("wide") & 1) == 0
        row = lax.broadcasted_iota(jnp.int32, (TILE, block_len), 0)
        powers = []
        for core, (avg, sq) in enumerate(((avg_ref[...], sq_ref[...]), (others_ref[0], others_ref[1]))):
            own = mine_ref[core * count:(core + 1) * count]
            other = got_ref[(1 - core) * count:(2 - core) * count]
            raws = []
            for total in (jnp.where(first_role, own, other), jnp.where(first_role, other, own)):
                mean_band = total / replicas
                avg = beta_one * avg + (1.0 - beta_one) * mean_band
                sq = beta_two * sq + (1.0 - beta_two) * mean_band * mean_band
                raws.append((avg / (jnp.sqrt(sq) + adam_eps)).reshape(rows, block_len))
            if core == 0:
                avg_out[...] = avg
                sq_out[...] = sq
            raw_out[core * rows:(core + 1) * rows, :] = jnp.where(first_role, raws[0], raws[1]).astype(jnp.bfloat16)
            powers.append([jnp.sum(raw * raw, axis=0, keepdims=True) for raw in raws])
        tile = jnp.zeros((TILE, block_len), jnp.float32)
        for step_index in range(STEPS):
            rest = powers[0][step_index] + powers[1][step_index]
            for part in range(3):
                piece = rest.astype(jnp.bfloat16).astype(jnp.float32)
                tile = jnp.where(row == STEPS * part + step_index, piece, tile)
                rest = rest - piece
        raw_out[2 * rows:, :] = tile.astype(jnp.bfloat16)

    return pl.pallas_call(
        kernel,
        in_specs=[VMEM] * 5,
        out_specs=[VMEM] * 3,
        out_shape=[pltpu.VMEM(flat, jnp.float32)] * 2 + [pltpu.VMEM((2 * rows + TILE, block_len), jnp.bfloat16)],
        compiler_params=SMALL,
        name="adam",
    )(*map(near_memory, (mine, got, exp_avg, exp_sq, others)))


def gathered(piece_refs, groups_ref, owners_ref, target, row, block, geometry):
    size, stride, owned, band_rows, row_blocks = geometry
    shift = (size // stride).bit_length() - 1
    owner, within = owner_of(owners_ref[row, block], owned)
    group = groups_ref[target & 1, owner ^ target]
    chip = group >> 1
    which = chip >> shift
    begin = (chip & ((1 << shift) - 1)) * stride + ((group & 1) * (row_blocks * owned) + row * owned + within) * band_rows
    rows = pl.ds(pl.multiple_of(begin, TILE), band_rows)
    value = piece_refs[0][rows, :]
    for number in range(1, len(piece_refs)):
        value = jnp.where(which == number, piece_refs[number][rows, :], value)
    return value


def exact_dot(values, table):
    length = values.shape[1]
    both = dot(values, table[:length])
    return both[:, :length] + both[:, length:]


def products_of(pieces, offsets, owners, columns, orders, band_rows, width):
    row_blocks, col_blocks = offsets.shape
    block_len = columns.shape[-1] // 2
    chunks = col_blocks // width
    geometry = (pieces[0].shape[0], 2 * pieces[0].shape[0] * len(pieces) >> len(orders[0]),
                col_blocks >> len(orders[0]), band_rows, row_blocks)

    def kernel(owners_ref, columns_ref, *refs):
        *piece_refs, out_ref, groups_ref = refs
        device = lax.axis_index("wide")
        fill_groups(groups_ref, orders)

        def body(part, carry):
            row, chunk = block_of(part, chunks, row_blocks)
            values = [gathered(piece_refs, groups_ref, owners_ref, device, row, chunk * width + index, geometry)
                      for index in range(width)]
            length = width * band_rows
            out_ref[pl.ds(pl.multiple_of(part * length, length), length), :] = exact_dot(
                jnp.concatenate(values, 0), columns_ref[0])
            return carry

        lax.fori_loop(0, row_blocks * chunks, body, 0)

    return pl.pallas_call(
        kernel,
        in_specs=[SMEM] + [VMEM] * (1 + len(pieces)),
        out_specs=VMEM,
        out_shape=pltpu.VMEM((row_blocks * col_blocks * band_rows, block_len), jnp.float32),
        scratch_shapes=[pltpu.SMEM((STEPS, 1 << len(orders[0])), jnp.int32)],
        compiler_params=SMALL,
        name="products_of",
    )(owners, *map(near_memory, (columns, *pieces)))


def weights_update(weights, own, products, other, tiles, count_all, offsets, owners, columns, ready, orders, band_rows, width):
    row_blocks, col_blocks = offsets.shape
    block_len = columns.shape[-1] // 2
    size = own[0].shape[0]
    pieces = len(own)
    stride = 2 * size * pieces >> len(orders[0])
    shards = tiles.shape[0] + 1
    geometry = (size, stride, col_blocks >> len(orders[0]), band_rows, row_blocks)
    chunks = col_blocks // width
    span = width * block_len
    count = len(ready)

    def kernel(offsets_ref, owners_ref, tiles_ref, weights_ref, columns_ref, products_ref, *refs):
        piece_refs = [refs[:pieces], refs[pieces:2 * pieces]]
        ready_refs = refs[2 * pieces:2 * pieces + count]
        refs = refs[2 * pieces + count:]
        out_hbm, scales_ref, ready_hbm = refs[0], refs[1], refs[2:2 + count]
        groups_ref, out_ref, departures, leaving, *scatters = refs[2 + count:]
        partner = lax.axis_index("wide") ^ 1
        first_role = (partner & 1) == 1
        copies = [
            pltpu.make_async_copy(source, target, leaving.at[index])
            for index, (source, target) in enumerate(zip(ready_refs, ready_hbm))
        ]
        for copy in copies:
            copy.start()
        fill_groups(groups_ref, orders)
        scatters = clear(scatters)
        scales = []
        rows = [[ref[begin + stride - TILE:begin + stride, :] for ref in piece_refs[0] for begin in range(0, size, stride)]]
        for shard in range(shards - 1):
            rows.append([tiles_ref[shard, group] for group in range(1 << len(orders[0]) - 1)])
        tile = tree_sum([axis_sum([value.astype(jnp.float32) for value in values], [order[:-1] for order in orders], first_role) for values in rows])
        parity = lax.broadcasted_iota(jnp.int32, tile.shape, 0) & 1
        for step_index in range(STEPS):
            power = jnp.sum(jnp.where(parity == step_index, tile, 0.0), keepdims=True)
            scales.append(jnp.broadcast_to(jnp.sqrt(power / count_all + rms_eps), (1, block_len)))
        inverses = [1.0 / scale for scale in scales]
        factors = [jnp.broadcast_to(factor, (band_rows, block_len)) for factor in (
            jnp.where(first_role, inverses[0], inverses[1]), jnp.where(first_role, inverses[1], inverses[0]))]

        def tile_of(part):
            row, chunk = block_of(part, chunks, row_blocks)
            return (pl.ds(pl.multiple_of(row * block_len, block_len), block_len),
                    pl.ds(pl.multiple_of(chunk * span, span), span))

        def departure(part):
            tile = tile_of(part)
            return pltpu.make_async_copy(out_ref.at[tile], out_hbm.at[tile], departures.at[part])

        def body(part, carry):
            row, chunk = block_of(part, chunks, row_blocks)
            values = [gathered(piece_refs[1], groups_ref, owners_ref, partner, row, chunk * width + index, geometry)
                      for index in range(width)]
            right = exact_dot(jnp.concatenate(values, 0), columns_ref[0])
            length = width * band_rows
            start = pl.multiple_of(part * length, length)
            ranges = [pl.ds(offsets_ref[row, chunk * width + index], band_rows) for index in range(width)]
            values = [
                products_ref[pl.ds(pl.multiple_of(start + index * band_rows, band_rows), band_rows), :] * factors[0]
                + right[index * band_rows:(index + 1) * band_rows] * factors[1] for index in range(width)]
            inverse = left_dot(columns_ref, scatters, ranges, values)
            tile = tile_of(part)
            out_ref[tile] = (weights_ref[tile].astype(jnp.float32) - learning_rate * inverse).astype(out_ref.dtype)
            departure(part).start()
            return carry

        lax.fori_loop(0, row_blocks * chunks, body, 0)
        for step_index in range(STEPS):
            scales_ref[step_index] = scales[step_index][0, 0]
        for part in range(row_blocks * chunks):
            departure(part).wait()
        for copy in copies:
            copy.wait()

    return pl.pallas_call(
        kernel,
        in_specs=[SMEM, SMEM] + [VMEM] * (4 + 2 * pieces + count),
        out_specs=[HBM, SMEM] + [HBM] * count,
        out_shape=[
            pltpu.HBM(weights.shape, weights.dtype),
            jax.ShapeDtypeStruct((STEPS,), jnp.float32),
        ] + [pltpu.HBM(value.shape, value.dtype) for value in ready],
        scratch_shapes=[
            pltpu.SMEM((STEPS, 1 << len(orders[0])), jnp.int32),
            pltpu.VMEM(weights.shape, weights.dtype),
            pltpu.SemaphoreType.DMA((row_blocks * chunks,)),
            pltpu.SemaphoreType.DMA((count,)),
        ] + [pltpu.VMEM((block_len, block_len), jnp.float32)] * (2 * width),
        compiler_params=SMALL,
        name="weights_update",
    )(offsets, owners, *map(near_memory, (tiles, weights, columns, products, *own, *other, *ready)))


def swap(value, orders, stage):
    pairs = [(index, index ^ (1 << orders[index & 1][stage])) for index in range(1 << len(orders[0]))]
    return lax.ppermute(value, "wide", pairs)


def across(value, orders, stage, shift, shards):
    pairs = []
    for index in range(1 << len(orders[0])):
        partner = index if stage is None else index ^ (1 << orders[index & 1][stage])
        pairs += [(index * shards + shard, partner * shards + (shard ^ shift)) for shard in range(shards)]
    return lax.ppermute(value, ("wide", "shard"), pairs)


def axis_sum(values, orders, first_role):
    sums = []
    for order in orders:
        entries = {}
        for place, value in enumerate(values):
            digits = [place >> (len(order) - 1 - position) & 1 for position in range(len(order))]
            entries[sum(digit << bit - 1 for digit, bit in zip(digits, order))] = value
        current = [entries[index] for index in range(len(values))]
        sums.append(tree_sum(current))
    return jnp.where(first_role, *sums)


def tree_sum(values):
    while len(values) > 1:
        values = [a + b for a, b in zip(values[::2], values[1::2])]
    return values[0]


def per_device(weights, momentum, grads, offsets, owners, exp_avg, exp_sq):
    row_blocks, owned, band_rows, block_len = exp_avg.shape
    replicas = lax.axis_size("wide")
    shards = lax.axis_size("shard")
    count_all = exp_avg.size * replicas * shards
    table = dct_table(block_len)
    picks = jnp.asarray(row_tables(table))
    columns = jnp.asarray(column_tables(table))
    width = 16
    bits = replicas.bit_length() - 1
    orders = [list(range(1, bits)) + [0] for _ in range(STEPS)]
    if bits > 3:
        orders[1][:2] = orders[1][1::-1]
    core = bits - 1
    near_momentum, near_grads, taken, kept, sent = bands(
        momentum[0], grads[:, 0], offsets, owners, picks, columns, band_rows, orders, 2 * width)
    new_momentum = momentum_update(near_momentum, near_grads, taken, offsets, columns, band_rows, width)
    middle = kept.shape[0] // 2
    high = swap(sent[middle:], orders, core)
    low = swap(sent[:middle], orders, core)
    send = kept[middle:] + high.astype(jnp.float32)
    low, _ = lax.optimization_barrier((low, send))
    keep = kept[:middle] + low.astype(jnp.float32)
    for stage in range(core):
        middle = send.shape[0] // 2
        if stage == core - 1:
            keep = keep + swap(send.astype(jnp.bfloat16), orders, stage).astype(jnp.float32)
            break
        high = swap(send[middle:].astype(jnp.bfloat16), orders, stage)
        low = swap(send[:middle].astype(jnp.bfloat16), orders, stage)
        send = keep[middle:] + high.astype(jnp.float32)
        low, _ = lax.optimization_barrier((low, send))
        keep = keep[:middle] + low.astype(jnp.float32)
    flat = (row_blocks * owned, band_rows, block_len)
    exp_avg_now, exp_sq_now = exp_avg.reshape(flat), exp_sq.reshape(flat)
    others = swap(jnp.stack([exp_avg_now, exp_sq_now]), orders, core)
    got = swap(keep, orders, core)
    avg_now, sq_now, raw = adam(keep, got, exp_avg_now, exp_sq_now, others, replicas)
    nears, fars = [], [raw]
    for stage in reversed(range(core)):
        nears = [jnp.concatenate(values, 0) if len(values) > 1 else values[0] for values in (nears, fars) if values]
        fars = []
        for value in nears:
            fars.append(swap(value, orders, stage))
    tiles = jnp.concatenate([value.reshape(-1, raw.shape[0], block_len)[:, -TILE:] for value in nears], 0)
    tiles = jnp.stack([
        jnp.concatenate([across(tiles, orders, turn, shift, shards) for turn in (None, 0)], 0)
        for shift in range(1, shards)])
    own = nears + fars
    other = [swap(value, orders, core) for value in own]
    products = products_of(own, offsets, owners, columns, orders, band_rows, 2 * width)
    new_weights, scales, new_momentum, avg_now, sq_now = weights_update(
        weights, own, products, other, tiles, count_all, offsets, owners, columns, (new_momentum, avg_now, sq_now), orders, band_rows, 2 * width)
    return (new_weights, new_momentum[None], avg_now.reshape(exp_avg.shape), sq_now.reshape(exp_sq.shape), scales)


def solution(mesh):
    in_specs = (
        P("shard", None),
        P("wide", "shard", None),
        P(None, "wide", "shard", None),
        P("shard", None),
        P("shard", None),
        P("shard", "wide", None, None),
        P("shard", "wide", None, None),
    )
    out_specs = (
        P("shard", None),
        P("wide", "shard", None),
        P("shard", "wide", None, None),
        P("shard", "wide", None, None),
        P(),
    )
    return jax.shard_map(per_device, mesh=mesh, in_specs=in_specs, out_specs=out_specs, check_vma=False)
```
